256 devices in a mesh: ctx: 32 (over y_hi, z, core), exp: 8 (over x, y_lo).
Axes of the slice: x: 4, y: 4 (y_hi: 2, y_lo: 2; y = y_hi * 2 + y_lo), z: 8, core: 2. Of those that a mesh axis runs over, the one named last changes fastest.
Arguments:
- queries: bfloat16 [4096, 6144], P('ctx', 'exp'), may hold values from -12 to 12
- keys_values: bfloat16 [4096, 8, 256], P('ctx', 'exp'), may hold values from -12 to 12
- doc_ids: int32 [4096], P('ctx'), may hold values from 0 to 7, never falling along the last dimension, each value on 1 to 3072 neighbouring positions
- gate_up: bfloat16 [8, 1280, 16384], P('exp', None, 'ctx'), may hold values from -6 to 6
- down_weight: bfloat16 [8, 16384, 6144], P('exp', 'ctx'), may hold values from -0.046875 to 0.046875
- routes: int32 [4096, 2], P(('ctx', 'exp')), may hold values from 0 to 7, all different within a row; in each aligned block of 16 rows (0 to 15, 16 to 31, ...) at most 5 rows name the same one
- route_weights: float32 [4096, 2], P(('ctx', 'exp')), may hold values from 0.1 to 1
Outputs:
- context: bfloat16 [4096, 6144], P('ctx', 'exp')
- moe_out: bfloat16 [4096, 6144], P(('ctx', 'exp'))
The draws below stay inside these ranges and needn't reach their ends.
Inputs may be any that keep to these rules, and one draw needn't show every extreme that they name: doc_ids never falls along the sequence; each document has 1 to 3072 tokens and one has exactly 3072. `routes`: the 2 experts of a token differ; among the 16 tokens of one device (aligned blocks) no expert is named more than 5 times, a bound that some block reaches.
All inputs are finite; a program needn't handle non-finite values.
Results may differ from the reference program's by a relative error of at most 0.025.
Values may be sent and summed in bfloat16 or wider, within the bound.
No kernel may reach another device: no remote copies, remote signals or barrier semaphores. Data moves between devices by JAX's collectives and lax.ppermute only.
A program may use at most 128 MiB of HBM per device.

```python
import math
import jax
import jax.numpy as jnp
import numpy as np
from jax import lax

D = 6144
FF = 16384
HQ = 48
KVH = 8
HD = 128
TOP = 2
DOCS = 8
EXPERTS = 8
SEQ = 4096
MOE_DEV = 16
CAP = 5
SLOTS = 1280
FF_DEV = 512
DOC_MOST = 3072


def base_values(key, shape):
    return jax.random.truncated_normal(key, -5.0, 5.0, shape, jnp.float32)


def draw_keys_values(key, part):
    own = jax.random.fold_in(key, 11)
    key_keys, key_values = jax.random.split(own, 2)
    keys = base_values(key_keys, (SEQ, KVH, HD))
    values = base_values(key_values, (SEQ, KVH, HD))
    return jnp.concatenate([keys, values], axis=-1).astype(jnp.bfloat16)


def draw_queries(key, part):
    own = jax.random.fold_in(key, 13)
    queries = base_values(own, (SEQ, HQ, HD))
    return queries.reshape(SEQ, HQ * HD).astype(jnp.bfloat16)


def with_spikes(array, own_key, source, target, parts, factor):
    owner, partner = [(jnp.arange(array.shape[dim]) // (array.shape[dim] // parts)).reshape([-1 if axis == dim else 1 for axis in range(array.ndim)]) for dim in (source, target)]
    chosen = jax.random.permutation(own_key, parts)[partner]
    strong = (owner == chosen) | (owner == (partner + parts // 2) % parts)
    return jnp.where(strong, factor * array, array)


def levels(stream_key, dims, cuts, least, top_value):
    factor_of = 1.0
    for axis_at, parts in cuts:
        steps = jax.random.uniform(jax.random.fold_in(jax.random.fold_in(stream_key, 6), axis_at), (parts,), jnp.float32, least / len(cuts), top_value / len(cuts))
        factor_of = factor_of * jnp.repeat(jnp.exp(steps), dims[axis_at] // parts).reshape((-1,) + (1,) * (len(dims) - 1 - axis_at))
    return factor_of


def length_profile(count, total, most, skew):
    loads = [(1 << 20) // math.isqrt(rank ** skew) + 1 for rank in range(2, count + 1)]
    rest, holding = total - most - (count - 1), [1] * (count - 1)
    while rest > 0:
        candidates = [i for i in range(count - 1) if holding[i] < most]
        mass, budget = sum([loads[i] for i in candidates]), rest
        for i in candidates:
            more = min(most - holding[i], max(1, budget * loads[i] // mass), rest)
            holding[i] = holding[i] + more
            rest = rest - more
    return np.array([most] + holding)


def uneven(rng, number_of, total, bound, slope):
    if number_of == 2:
        one = jax.random.randint(rng, (), max(1, total - bound), min(bound, total - 1) + 1)
        return jnp.stack([one, total - one])
    sizes = jnp.asarray(length_profile(number_of, total, bound, slope), jnp.int32)
    pairs = (number_of - 1) // 2
    source_of, receiver = sizes[1:1 + 2 * pairs:2], sizes[2:2 + 2 * pairs:2]
    room = jnp.minimum(source_of - 1, bound - receiver)
    passed = jax.random.randint(jax.random.fold_in(rng, 1), (pairs,), 0, 1 << 20) % (room + 1)
    sizes = sizes.at[1:1 + 2 * pairs:2].set(source_of - passed).at[2:2 + 2 * pairs:2].set(receiver + passed)
    return sizes[jax.random.permutation(jax.random.fold_in(rng, 2), number_of)]


def deal_out(rng, own, number, rows, amount, top, bound, skew):
    order = jax.random.permutation(rng, amount)
    packed, usual = portions_of(amount, rows * top, bound, skew, True), portions_of(amount, rows * top, bound, skew, False)
    places = jnp.arange(amount)

    def named(tallies, rotation):
        used = int((tallies > 0).sum())
        fixed = max(1, used // 4)
        shifted = fixed + (places - fixed + rotation * (used - fixed)) % max(1, amount - fixed)
        return jnp.zeros((amount,), jnp.int32).at[order[jnp.where(places < fixed, places, shifted)]].set(jnp.asarray(tallies, jnp.int32))

    tallies = jnp.where(number % 4 == 0, named(packed, number // 4), named(usual, number - number // 4 - 1))
    mixed = jax.random.permutation(jax.random.fold_in(own, 3), amount)
    donor, receiver = mixed[0:amount // 2 * 2:2], mixed[1:amount // 2 * 2:2]
    room = jnp.minimum(tallies[donor] - 1, bound - tallies[receiver]) // 2
    room = jnp.where((donor == order[0]) | (receiver == order[0]) | (tallies[receiver] == 0), 0, jnp.maximum(room, 0))
    shifted = jax.random.randint(jax.random.fold_in(own, 4), (amount // 2,), 0, 1 << 20) % (room + 1)
    tallies = tallies.at[donor].add(-shifted).at[receiver].add(shifted)
    items = jnp.searchsorted(jnp.cumsum(tallies), jnp.arange(rows * top), side="right").astype(jnp.int32)
    grid = items.reshape(top, rows).T
    grid = grid[jax.random.permutation(jax.random.fold_in(own, 1), rows)]
    rotation = jax.random.randint(jax.random.fold_in(own, 2), (rows, 1), 0, top)
    return jnp.take_along_axis(grid, (jnp.arange(top)[None, :] + rotation) % top, axis=1)


def portions_of(amount, total, most, skew, full):
    loads = [(1 << 20) // math.isqrt(grade ** skew) + 1 for grade in range(1, amount + 1)]
    largest = most if full else min(most, max(-(-total // amount), total * loads[0] // sum(loads)))
    least = 1 if total - largest >= amount - 1 else 0
    holding, surplus = [largest] + [least] * (amount - 1), total - largest - least * (amount - 1)
    while surplus > 0:
        movable = [i for i in range(1, amount) if holding[i] < largest] or [i for i in range(1, amount) if holding[i] < most]
        pool, remaining = sum([loads[i] for i in movable]), surplus
        for i in movable:
            more = min(most - holding[i], max(1, remaining * loads[i] // pool), surplus)
            holding[i] = holding[i] + more
            surplus = surplus - more
    return np.array(holding)


def gaussian(own_key, dims, deviation, bound, cuts=(), kind=jnp.bfloat16):
    array = jax.random.normal(own_key, dims, jnp.float32) * deviation
    if len(cuts) > 0:
        array = levels(own_key, dims, cuts, -0.22, 0.18) * array
    return jnp.clip(array, min=-bound, max=bound).astype(kind)


def bell_draw_with(own_key, dims, deviation, most, pieces, heavy, kind=jnp.bfloat16):
    values = deviation * jax.random.normal(own_key, dims, jnp.float32)
    if pieces:
        values = values * levels(own_key, dims, pieces, -0.22, 0.18)
    return jnp.clip(with_spikes(values, jax.random.fold_in(own_key, 3), *heavy), -most, most).astype(kind)


def setup_inputs(seed: int = 0) -> dict:
    splits = jax.random.split(jax.random.key(seed), 8)
    queries = draw_queries(jax.random.fold_in(splits[7], 71), 0)
    keys_values = draw_keys_values(jax.random.fold_in(splits[7], 71), 0)
    doc_ids = jnp.searchsorted(jnp.cumsum(uneven(splits[2], DOCS, SEQ, DOC_MOST, 0)), jnp.arange(SEQ), side="right").astype(jnp.int32)
    gate_up = bell_draw_with(splits[3], (EXPERTS, SLOTS, FF), 1.0, 6.0, ((0, 8), (2, 32)), (2, 1, 32, 2.75))
    down_weight = gaussian(splits[4], (EXPERTS, FF, D), FF ** -0.5, 0.046875, ((0, 8), (1, 32)))
    routes_keys = jax.random.split(jax.random.fold_in(splits[5], 1), SEQ // MOE_DEV)
    routes_turns = jax.random.permutation(jax.random.fold_in(splits[5], 3), SEQ // MOE_DEV)
    routes = jax.vmap(lambda own, number: deal_out(jax.random.fold_in(splits[5], 2), own, number, MOE_DEV, EXPERTS, TOP, CAP, 2))(routes_keys, routes_turns).reshape((SEQ, TOP))
    route_weights = jnp.clip(jnp.exp(math.log(1.0) - 2.3025851 * jax.random.uniform(splits[6], (SEQ, TOP), jnp.float32) ** levels(splits[6], (SEQ, TOP), ((0, 256),), -0.2, 0.2)), 0.1, 1.0)
    return {"queries": queries, "keys_values": keys_values, "doc_ids": doc_ids, "gate_up": gate_up, "down_weight": down_weight, "routes": routes, "route_weights": route_weights}


def attention(queries, keys_values, doc_ids):
    groups = HQ // KVH
    blk = math.gcd(SEQ, 512)
    keys = keys_values[:, :, :HD].astype(jnp.float32)
    values = keys_values[:, :, HD:].astype(jnp.float32)
    positions = jnp.arange(SEQ, dtype=jnp.int32)
    scale = 1.0 / math.sqrt(HD)

    def attend(index):
        start = (index * blk).astype(jnp.int32)
        query_blk = lax.dynamic_slice_in_dim(queries, start, blk, 0).astype(jnp.float32).reshape(blk, KVH, groups, HD)
        doc_blk = lax.dynamic_slice_in_dim(doc_ids, start, blk, 0)
        pos_blk = start + jnp.arange(blk, dtype=jnp.int32)
        scores = jnp.einsum('qhgd,khd->hgqk', query_blk, keys) * scale
        allowed = (doc_blk[:, None] == doc_ids[None, :]) & (positions[None, :] <= pos_blk[:, None])
        scores = jnp.where(allowed, scores, jnp.float32(-1e+30))
        row_max = lax.optimization_barrier(jnp.max(scores, axis=-1, keepdims=True))
        weights = jnp.where(allowed, jnp.exp(scores - row_max), jnp.float32(0.0))
        denominator = lax.optimization_barrier(jnp.sum(weights, axis=-1))
        rounded = lax.optimization_barrier(weights.astype(jnp.bfloat16)).astype(jnp.float32)
        summed = jnp.einsum('hgqk,khd->qhgd', rounded, values)
        result = summed / jnp.transpose(denominator, (2, 0, 1))[..., None]
        return result.reshape(blk, HQ * HD).astype(jnp.bfloat16)
    blocks = lax.map(attend, jnp.arange(SEQ // blk, dtype=jnp.int32))
    return blocks.reshape(SEQ, HQ * HD)

def experts_out(gate_up, down_weight, routes, route_weights):
    spans = FF // FF_DEV

    def one_expert(expert):
        acts = gate_up[expert]
        weight = down_weight[expert]

        def step(total, span):
            start = (span * FF_DEV).astype(jnp.int32)
            acts_part = lax.dynamic_slice_in_dim(acts, start, FF_DEV, 1)
            weight_part = lax.dynamic_slice_in_dim(weight, start, FF_DEV, 0)
            part = jnp.dot(acts_part, weight_part, preferred_element_type=jnp.float32)
            part = lax.optimization_barrier(part.astype(jnp.bfloat16))
            return (total + part.astype(jnp.float32), None)
        total, _ = lax.scan(step, jnp.zeros((SLOTS, D), jnp.float32), jnp.arange(spans, dtype=jnp.int32))
        return total.astype(jnp.bfloat16)
    expert_rows = lax.map(one_expert, jnp.arange(EXPERTS, dtype=jnp.int32))
    flat = routes.reshape(SEQ // MOE_DEV, MOE_DEV * TOP)
    onehot = (flat[..., None] == jnp.arange(EXPERTS, dtype=jnp.int32)).astype(jnp.int32)
    earlier = jnp.cumsum(onehot, axis=1) - onehot
    slot = lax.optimization_barrier(jnp.sum(earlier * onehot, axis=-1)).reshape(SEQ, TOP)
    source = jnp.arange(SEQ, dtype=jnp.int32) // MOE_DEV
    row_index = source[:, None] * CAP + slot
    picked = expert_rows[routes, row_index].astype(jnp.float32)
    return lax.optimization_barrier(jnp.sum(route_weights[:, :, None] * picked, axis=1))

def reference(queries, keys_values, doc_ids, gate_up, down_weight, routes, route_weights):
    context = attention(queries, keys_values, doc_ids)
    mixed = experts_out(gate_up, down_weight, routes, route_weights)
    moe_out = (context.astype(jnp.float32) + mixed).astype(jnp.bfloat16)
    return (context, moe_out)
```

```python
import math

import jax
import jax.numpy as jnp
from jax import lax
from jax.experimental import pallas as pl
from jax.experimental.pallas import tpu as pltpu
from jax.sharding import Mesh
from jax.sharding import PartitionSpec as P

AXES = ("yh", "z", "c", "x", "yl")
SHAPE = (2, 8, 2, 4, 2)
CTX = ("yh", "z", "c")
EXP = ("x", "yl")
Z = 8
EXPERTS = 8
PAD = 16
GROUPS = 2
PIECES = 4
PRODUCT_VMEM = 16 * 1024 * 1024
ATTENTION_VMEM = 24 * 1024 * 1024


def shift(value, step):
    return lax.ppermute(value, "z", [(i, (i + step) % Z) for i in range(Z)])


def swap(value, axis):
    return lax.ppermute(value, axis, [(0, 1), (1, 0)])


def after(value, *earlier):
    return lax.optimization_barrier((value,) + earlier)[0]


def attention_kernel(head, place, q_ref, doc_ref, a_ref, b_ref, o_ref, q_all, scores, top, total, acc):
    tokens = q_ref.shape[0]
    groups = q_ref.shape[1] // head
    high, along, core = place[0], place[1], place[2]
    mine = (high * Z + along) * 2 + core
    for g in range(groups):
        q_all[g * tokens : (g + 1) * tokens, :] = q_ref[:, g * head : (g + 1) * head]
    row = doc_ref[...].astype(jnp.float32)
    query_docs = jnp.transpose(jnp.broadcast_to(row, (tokens, tokens)))
    query_pos = lax.broadcasted_iota(jnp.int32, (tokens, tokens), 0) + mine * tokens
    lane = lax.broadcasted_iota(jnp.int32, (tokens, tokens), 1)
    top[...] = jnp.full_like(top, -1e30)
    total[...] = jnp.zeros_like(total)
    acc[...] = jnp.zeros_like(acc)
    arrays = ((a_ref, 0), (b_ref, 1))

    def origin(k, other_core):
        other_high = lax.rem(k, 2)
        high_at = high + other_high - 2 * high * other_high
        core_at = core + other_core - 2 * core * other_core
        return (high_at * Z + lax.div(k, 2)) * 2 + core_at

    for n, (ref, other_core) in enumerate(arrays):

        def score(k, carry, ref=ref, n=n, other_core=other_core):
            where = origin(k, other_core)

            @pl.when(where <= mine)
            def _():
                docs = ref[k, tokens : tokens + PAD, :tokens].astype(jnp.float32)[:1]
                allowed = (docs == query_docs) & (where * tokens + lane <= query_pos)
                s = lax.dot_general(
                    q_all[...],
                    ref[k, :tokens, :head],
                    (((1,), (1,)), ((), ())),
                    preferred_element_type=jnp.float32,
                )
                s = s.reshape(groups, tokens, tokens)
                s = jnp.where(allowed[None], s, jnp.float32(-1e30)).reshape(groups * tokens, tokens)
                scores[n * 2 * Z + k] = s
                top[...] = jnp.maximum(top[...], s)

            return carry

        lax.fori_loop(0, 2 * Z, score, 0)
    top[...] = jnp.broadcast_to(jnp.max(top[...], axis=1, keepdims=True), top.shape)
    factor = math.log2(math.e) / math.sqrt(head)
    for n, (ref, other_core) in enumerate(arrays):

        def mix(k, carry, ref=ref, n=n, other_core=other_core):
            where = origin(k, other_core)

            @pl.when(where <= mine)
            def _():
                weights = jnp.exp2((scores[n * 2 * Z + k] - top[...]) * factor)
                total[...] += weights
                acc[...] += jnp.dot(
                    weights.astype(jnp.bfloat16),
                    ref[k, :tokens, head:],
                    preferred_element_type=jnp.float32,
                )

            return carry

        lax.fori_loop(0, 2 * Z, mix, 0)
    out = acc[...] / jnp.sum(total[...], axis=1, keepdims=True)
    out = out.astype(o_ref.dtype)
    for g in range(groups):
        o_ref[:, g * head : (g + 1) * head] = out[g * tokens : (g + 1) * tokens, :]


def key_block(keys_values, doc_ids):
    tokens, width = doc_ids.shape[0], keys_values.shape[2]
    docs = jnp.pad(doc_ids.astype(jnp.bfloat16)[None, :], ((0, PAD - 1), (0, width - tokens)))
    return jnp.concatenate([keys_values, docs[:, None, :]], axis=0)


def attend(place, queries, doc_ids, near, far):
    tokens, width = doc_ids.shape[0], near.shape[-1]
    head = width // 2
    rows = queries.shape[1] // head * tokens
    spec = pl.BlockSpec(memory_space=pltpu.VMEM)
    return pl.pallas_call(
        lambda *refs: attention_kernel(head, *refs),
        out_shape=jax.ShapeDtypeStruct(queries.shape, jnp.bfloat16),
        in_specs=[pl.BlockSpec(memory_space=pltpu.SMEM)] + [spec] * 4,
        out_specs=spec,
        scratch_shapes=[
            pltpu.VMEM((rows, head), jnp.bfloat16),
            pltpu.VMEM((4 * Z, rows, tokens), jnp.float32),
            pltpu.VMEM((rows, tokens), jnp.float32),
            pltpu.VMEM((rows, tokens), jnp.float32),
            pltpu.VMEM((rows, head), jnp.float32),
        ],
        compiler_params=pltpu.CompilerParams(vmem_limit_bytes=ATTENTION_VMEM),
        name="attention",
    )(place, queries, doc_ids[None, :], near, far)


def product_kernel(place, a_ref, b_ref, wa_ref, wb_ref, o_ref):
    depth = a_ref.shape[-1]
    out = jnp.dot(a_ref[...].reshape(-1, depth), wa_ref[...], preferred_element_type=jnp.float32)
    out += jnp.dot(b_ref[...].reshape(-1, depth), wb_ref[...], preferred_element_type=jnp.float32)
    o_ref[...] = out.astype(o_ref.dtype).reshape(o_ref.shape)


def product(place, acts, acts_other, weight, other, first, tile, tiles, block, steps, pick):
    depth, rows = acts.shape[-1], acts.shape[2]
    half, start = weight.shape[1] // (2 * tile), first % (other.shape[1] // tile)
    acts_spec = pl.BlockSpec(block + (rows, depth), lambda j, i, s: pick(i, s) + (0, 0))
    return pl.pallas_call(
        product_kernel,
        out_shape=jax.ShapeDtypeStruct((steps * block[0], block[1], rows, tiles * tile), jnp.bfloat16),
        grid_spec=pltpu.PrefetchScalarGridSpec(
            num_scalar_prefetch=1,
            grid=(tiles, steps),
            in_specs=[
                acts_spec,
                acts_spec,
                pl.BlockSpec((depth, tile), lambda j, i, s: (0, s[2] * half + first + j)),
                pl.BlockSpec((depth, tile), lambda j, i, s: (0, start + j)),
            ],
            out_specs=pl.BlockSpec(block + (rows, tile), lambda j, i, s: (i, 0, 0, j)),
        ),
        compiler_params=pltpu.CompilerParams(vmem_limit_bytes=PRODUCT_VMEM),
        name="product",
    )(place, acts, acts_other, weight, other)


def add(*terms):
    total = terms[0].astype(jnp.float32)
    for term in terms[1:]:
        total = total + term.astype(jnp.float32)
    return total.astype(jnp.bfloat16)


def join(*values):
    return lax.optimization_barrier(values)


def chunk(array, at, axis):
    return lax.dynamic_index_in_dim(array, at % Z, axis, keepdims=False)


def shards(queries, keys_values, doc_ids, gate_up, down_weight, routes, route_weights):
    high, along, core = (lax.axis_index(name).astype(jnp.int32) for name in CTX)
    place = jnp.stack([high, along, core])
    weight = down_weight[0]
    columns = weight.shape[1] // (2 * GROUPS)
    depth = weight.shape[0]
    acts = gate_up[0].reshape(2, Z, -1, depth)

    acts_other = swap(gate_up[0], "c")
    part = lax.dynamic_slice(weight, (0, (1 - core) * GROUPS * columns), (depth, columns))
    other = [swap(part, "c")]
    block = key_block(keys_values, doc_ids)
    block_other = swap(block, "yh")
    at = after(((1 - core) * GROUPS + 1) * columns, part, block)
    other.append(swap(lax.dynamic_slice(weight, (0, at), (depth, columns)), "c"))
    acts_other, other[0], block_other = join(acts_other, other[0], block_other)
    acts_other = acts_other.reshape(2, Z, -1, depth)
    near = lax.all_gather(jnp.concatenate([block, block_other], axis=0), "z", axis=0, tiled=True)

    def first_group(where, block, steps, pick):
        return product(where, acts, acts_other, weight, other[0], 0, columns // 2, 2, block, steps, pick)

    def second_group(where, piece, pieces, pick):
        tile = columns // PIECES
        return product(
            where, acts, acts_other, weight, other[1], PIECES + piece, tile, pieces, (1, Z), 1, pick
        )[0]

    def sent_piece(where, piece):
        return second_group(where, piece, 1, lambda i, s: (1 - s[0], 0))

    down = first_group(place, (2, 1), 1, lambda i, s: (0, (s[1] + 4) % Z))[:, 0]
    up = first_group(after(place, down), (2, 1), 1, lambda i, s: (0, (s[1] + 3) % Z))[:, 0]
    sent = sent_piece(after(place, up), 0)
    down, up, sent = join(down, up, sent)
    got = []

    down, up, piece = shift(down, -1), shift(up, 1), swap(sent, "yh")
    full = first_group(after(place, sent), (1, Z), 2, lambda i, s: (i, 0))
    sent = sent_piece(after(place, full), 1)
    down, up, piece, full, sent = join(down, up, piece, full, sent)
    got.append(piece)
    down = add(down, chunk(full, along + 5, 1))
    up = add(up, chunk(full, along + 2, 1))
    down, up, sent = join(down, up, sent)

    here = after(place, down)
    down, up, piece = shift(down, -1), shift(up, 1), swap(sent, "yh")
    sent = sent_piece(here, 2)
    kept = second_group(after(place, sent), 0, PIECES, lambda i, s: (s[0], 0))
    down, up, piece, kept, sent = join(down, up, piece, kept, sent)
    got.append(piece)
    down = add(down, chunk(full, along + 6, 1))
    up = add(up, chunk(full, along + 1, 1))
    down, up, sent = join(down, up, sent)

    here = after(place, down)
    down, up, piece = shift(down, -1), shift(up, 1), swap(sent, "yh")
    sent = sent_piece(here, 3)
    down, up, piece, sent = join(down, up, piece, sent)
    got.append(piece)
    down = add(down, chunk(full, along + 7, 1))
    down, sent = join(down, sent)

    down, piece = shift(down, -1), swap(sent, "yh")
    down, piece, near = join(down, piece, near)
    got.append(piece)
    first = add(down, up, chunk(full, along, 1))

    def second_term(offset):
        received = jnp.concatenate([chunk(piece, along + offset, 0) for piece in got], axis=1)
        return chunk(kept, along + offset, 0), received

    going = chunk_of(first, 1 - high)
    down, up = add(*second_term(4)), add(*second_term(3))
    down, up, going = join(down, up, going)
    down, up, moved = shift(down, -1), shift(up, 1), swap(going, "yh")
    near = near.reshape(2 * Z, -1, near.shape[-1])
    context = attend(place, queries, doc_ids, near, swap(near, "c"))
    down, up, context = join(down, up, context)
    residual = lax.all_to_all(context, EXP, split_axis=0, concat_axis=1, tiled=True)
    down, up = add(down, *second_term(5)), add(up, *second_term(2))
    down, up = shift(down, -1), shift(up, 1)
    down, up, moved = join(down, up, moved)
    first = add(chunk_of(first, high), moved)
    down, up = add(down, *second_term(6)), add(up, *second_term(1))
    down, up = shift(down, -1), shift(up, 1)
    down, up, residual = join(down, up, residual)
    down = add(down, *second_term(7))
    second = add(shift(down, -1), up, *second_term(0))

    tokens = routes.shape[0]
    capacity = first.shape[0] // (2 * EXPERTS)
    mix = mixing(routes, route_weights, capacity)
    mixed = []
    for rows in (first, second):
        home = lax.all_to_all(
            rows.reshape(2 * EXPERTS, capacity, -1), ("c",) + EXP, split_axis=0, concat_axis=0, tiled=True
        )
        home = home.reshape(2, EXPERTS * capacity, -1)
        both = jnp.einsum("tr,crn->tcn", mix, home, preferred_element_type=jnp.float32)
        mixed.append(both[:tokens] + both[tokens:])
    mixed = jnp.concatenate(mixed, axis=2).reshape(tokens, -1)
    moe_out = residual.astype(jnp.float32) + mixed
    return (context, moe_out.astype(jnp.bfloat16))


def chunk_of(array, at):
    return lax.dynamic_index_in_dim(array, at, 0, keepdims=False)


def mixing(routes, route_weights, capacity):
    flat = routes.reshape(-1)
    pairs = jnp.arange(flat.shape[0])
    same = (flat[:, None] == flat[None, :]) & (pairs[None, :] < pairs[:, None])
    slot = jnp.sum(same.astype(jnp.int32), axis=1).reshape(routes.shape)
    row = routes * capacity + slot
    hit = row[:, :, None] == jnp.arange(EXPERTS * capacity)[None, None, :]
    mix = jnp.sum(jnp.where(hit, route_weights[:, :, None], 0.0), axis=1)
    coarse = mix.astype(jnp.bfloat16)
    fine = (mix - coarse.astype(jnp.float32)).astype(jnp.bfloat16)
    return jnp.concatenate([coarse, fine], axis=0)


def solution(mesh):
    inner = Mesh(mesh.devices.reshape(SHAPE), AXES)
    in_specs = (
        P(CTX, EXP),
        P(CTX, EXP, None),
        P(CTX),
        P(EXP, None, CTX),
        P(EXP, CTX, None),
        P(CTX + EXP, None),
        P(CTX + EXP, None),
    )
    out_specs = (P(CTX, EXP), P(CTX + EXP, None))
    return jax.shard_map(shards, mesh=inner, in_specs=in_specs, out_specs=out_specs, check_vma=False)
```

```python
import math

import jax
import jax.numpy as jnp
from jax import lax
from jax.experimental import pallas as pl
from jax.experimental.pallas import tpu as pltpu
from jax.sharding import Mesh
from jax.sharding import PartitionSpec as P

AXES = ("yh", "z", "c", "x", "yl")
SHAPE = (2, 8, 2, 4, 2)
CTX = ("yh", "z", "c")
EXP = ("x", "yl")
Z = 8
EXPERTS = 8
PAD = 16
GROUPS = 2
ORDER = (4, 3, 5, 2, 6, 1, 7, 0)
PRODUCT_VMEM = 16 * 1024 * 1024
ATTENTION_VMEM = 24 * 1024 * 1024


def shift(value, step):
    return lax.ppermute(value, "z", [(i, (i + step) % Z) for i in range(Z)])


def swap(value, axis):
    return lax.ppermute(value, axis, [(0, 1), (1, 0)])


def after(value, *earlier):
    return lax.optimization_barrier((value,) + earlier)[0]


def attention_kernel(head, place, q_ref, doc_ref, a_ref, b_ref, o_ref, q_all, scores, top, total, acc):
    tokens = q_ref.shape[0]
    groups = q_ref.shape[1] // head
    high, along, core = place[0], place[1], place[2]
    mine = (high * Z + along) * 2 + core
    for g in range(groups):
        q_all[g * tokens : (g + 1) * tokens, :] = q_ref[:, g * head : (g + 1) * head]
    row = doc_ref[...].astype(jnp.float32)
    query_docs = jnp.transpose(jnp.broadcast_to(row, (tokens, tokens)))
    query_pos = lax.broadcasted_iota(jnp.int32, (tokens, tokens), 0) + mine * tokens
    lane = lax.broadcasted_iota(jnp.int32, (tokens, tokens), 1)
    top[...] = jnp.full_like(top, -1e30)
    total[...] = jnp.zeros_like(total)
    acc[...] = jnp.zeros_like(acc)
    arrays = ((a_ref, 0), (b_ref, 1))

    def origin(k, other_core):
        other_high = lax.rem(k, 2)
        high_at = high + other_high - 2 * high * other_high
        core_at = core + other_core - 2 * core * other_core
        return (high_at * Z + lax.div(k, 2)) * 2 + core_at

    for n, (ref, other_core) in enumerate(arrays):

        def score(k, carry, ref=ref, n=n, other_core=other_core):
            where = origin(k, other_core)

            @pl.when(where <= mine)
            def _():
                docs = ref[k, tokens : tokens + PAD, :tokens].astype(jnp.float32)[:1]
                allowed = (docs == query_docs) & (where * tokens + lane <= query_pos)
                s = lax.dot_general(
                    q_all[...],
                    ref[k, :tokens, :head],
                    (((1,), (1,)), ((), ())),
                    preferred_element_type=jnp.float32,
                )
                s = s.reshape(groups, tokens, tokens)
                s = jnp.where(allowed[None], s, jnp.float32(-1e30)).reshape(groups * tokens, tokens)
                scores[n * 2 * Z + k] = s
                top[...] = jnp.maximum(top[...], s)

            return carry

        lax.fori_loop(0, 2 * Z, score, 0)
    top[...] = jnp.broadcast_to(jnp.max(top[...], axis=1, keepdims=True), top.shape)
    factor = math.log2(math.e) / math.sqrt(head)
    for n, (ref, other_core) in enumerate(arrays):

        def mix(k, carry, ref=ref, n=n, other_core=other_core):
            where = origin(k, other_core)

            @pl.when(where <= mine)
            def _():
                weights = jnp.exp2((scores[n * 2 * Z + k] - top[...]) * factor)
                total[...] += weights
                acc[...] += jnp.dot(
                    weights.astype(jnp.bfloat16),
                    ref[k, :tokens, head:],
                    preferred_element_type=jnp.float32,
                )

            return carry

        lax.fori_loop(0, 2 * Z, mix, 0)
    out = acc[...] / jnp.sum(total[...], axis=1, keepdims=True)
    out = out.astype(o_ref.dtype)
    for g in range(groups):
        o_ref[:, g * head : (g + 1) * head] = out[g * tokens : (g + 1) * tokens, :]


def key_block(keys_values, doc_ids):
    tokens, width = doc_ids.shape[0], keys_values.shape[2]
    docs = jnp.pad(doc_ids.astype(jnp.bfloat16)[None, :], ((0, PAD - 1), (0, width - tokens)))
    return jnp.concatenate([keys_values, docs[:, None, :]], axis=0)


def attend(place, queries, doc_ids, near, far):
    tokens, width = doc_ids.shape[0], near.shape[-1]
    head = width // 2
    rows = queries.shape[1] // head * tokens
    spec = pl.BlockSpec(memory_space=pltpu.VMEM)
    return pl.pallas_call(
        lambda *refs: attention_kernel(head, *refs),
        out_shape=jax.ShapeDtypeStruct(queries.shape, jnp.bfloat16),
        in_specs=[pl.BlockSpec(memory_space=pltpu.SMEM)] + [spec] * 4,
        out_specs=spec,
        scratch_shapes=[
            pltpu.VMEM((rows, head), jnp.bfloat16),
            pltpu.VMEM((4 * Z, rows, tokens), jnp.float32),
            pltpu.VMEM((rows, tokens), jnp.float32),
            pltpu.VMEM((rows, tokens), jnp.float32),
            pltpu.VMEM((rows, head), jnp.float32),
        ],
        compiler_params=pltpu.CompilerParams(vmem_limit_bytes=ATTENTION_VMEM),
        name="attention",
    )(place, queries, doc_ids[None, :], near, far)


def slice_kernel(place, weight_ref, *refs):
    outs, sems = refs[:-1], refs[-1]
    columns, strip = outs[0].shape[1], outs[0].shape[0] // 2
    copies = []
    for i, out in enumerate(outs):
        at = pl.multiple_of(((1 - place[2]) * len(outs) + i) * columns, columns)
        for k in range(2):
            rows = pl.ds(k * strip, strip)
            copies.append(
                pltpu.make_async_copy(weight_ref.at[rows, pl.ds(at, columns)], out.at[rows, :], sems.at[2 * i + k])
            )
    for copy in copies:
        copy.start()
    for copy in copies:
        copy.wait()


def other_columns(place, weight, columns):
    any_spec = pl.BlockSpec(memory_space=pl.ANY)
    return pl.pallas_call(
        slice_kernel,
        out_shape=[jax.ShapeDtypeStruct((weight.shape[0], columns), weight.dtype)] * GROUPS,
        in_specs=[pl.BlockSpec(memory_space=pltpu.SMEM), any_spec],
        out_specs=[any_spec] * GROUPS,
        scratch_shapes=[pltpu.SemaphoreType.DMA((2 * GROUPS,))],
        name="columns",
    )(place, weight)


def product_kernel(count, offsets, place, *refs):
    depth = refs[0].shape[-1]
    wa_ref, wb_ref = refs[2 * count : 2 * count + 2]
    a = jnp.concatenate([ref[...].reshape(-1, depth) for ref in refs[:count]], axis=0)
    b = jnp.concatenate([ref[...].reshape(-1, depth) for ref in refs[count : 2 * count]], axis=0)
    out = jnp.dot(a, wa_ref[...], preferred_element_type=jnp.float32)
    out += jnp.dot(b, wb_ref[...], preferred_element_type=jnp.float32)
    out = out.astype(jnp.bfloat16)
    if offsets is None:
        o_refs = refs[2 * count + 2 :]
        rows = out.shape[0] // len(o_refs)
        for i, o_ref in enumerate(o_refs):
            o_ref[...] = out[i * rows : (i + 1) * rows].reshape(o_ref.shape)
    else:
        o_refs, chunks = refs[2 * count + 2 : -1], refs[-1]
        chunks[...] = out.reshape(chunks.shape)
        for o_ref, picks in zip(o_refs, offsets):
            for k, offset in enumerate(picks):
                o_ref[k] = chunks[lax.rem(place[1] + offset, Z)].reshape(o_ref.shape[1:])


def product(place, acts, acts_other, weight, other, first, block, picks, steps, offsets, split):
    depth, rows = acts.shape[-1], acts.shape[2]
    columns = other.shape[1]
    tile = columns // 2
    half, start = weight.shape[1] // (2 * tile), first * 2
    specs = [pl.BlockSpec(block + (rows, depth), lambda j, i, s, pick=pick: pick(i, s) + (0, 0)) for pick in picks]
    if offsets is None:
        shapes, blocks = [block + (rows, columns)] * len(picks), [block + (rows, tile)] * len(picks)
        scratch = []
    else:
        split = (steps,) if split else ()
        shapes = [(len(o),) + split + (rows, columns) for o in offsets]
        blocks = [(len(o),) + (1,) * len(split) + (rows, tile) for o in offsets]
        scratch = [pltpu.VMEM(block[1:] + (rows, tile), jnp.bfloat16)]

    def out_map(rank):
        if rank == 3:
            return lambda j, i, s: (0, 0, j)
        return lambda j, i, s: (0, i, 0, j)

    weight = pltpu.with_memory_space_constraint(weight, pltpu.HBM)
    return pl.pallas_call(
        lambda *refs: product_kernel(len(picks), offsets, *refs),
        out_shape=[jax.ShapeDtypeStruct(shape, jnp.bfloat16) for shape in shapes],
        grid_spec=pltpu.PrefetchScalarGridSpec(
            num_scalar_prefetch=1,
            grid=(2, steps),
            in_specs=specs
            + specs
            + [
                pl.BlockSpec((depth, tile), lambda j, i, s: (0, s[2] * half + start + j)),
                pl.BlockSpec((depth, tile), lambda j, i, s: (0, j)),
            ],
            out_specs=[pl.BlockSpec(b, out_map(len(b))) for b in blocks],
            scratch_shapes=scratch,
        ),
        compiler_params=pltpu.CompilerParams(vmem_limit_bytes=PRODUCT_VMEM),
        name="product",
    )(place, *([acts] * len(picks)), *([acts_other] * len(picks)), weight, other)


def add(*terms):
    total = terms[0].astype(jnp.float32)
    for term in terms[1:]:
        total = total + term.astype(jnp.float32)
    return total.astype(jnp.bfloat16)


def join(*values):
    return lax.optimization_barrier(values)


def shards(queries, keys_values, doc_ids, gate_up, down_weight, routes, route_weights):
    high, along, core = (lax.axis_index(name).astype(jnp.int32) for name in CTX)
    place = jnp.stack([high, along, core])
    weight = down_weight[0]
    columns = weight.shape[1] // (2 * GROUPS)
    depth = weight.shape[0]
    acts = gate_up[0].reshape(2, Z, -1, depth)

    acts_other = swap(gate_up[0], "c")
    parts = other_columns(place, weight, columns)
    other = [swap(part, "c") for part in parts]
    block = key_block(keys_values, after(doc_ids, *parts))
    block_other = swap(block, "yh")
    acts_other, other[0], block_other = join(acts_other, other[0], block_other)
    acts_other = acts_other.reshape(2, Z, -1, depth)
    near = lax.all_gather(jnp.concatenate([block, block_other], axis=0), "z", axis=0, tiled=True)

    def make(where, group, block, picks, steps=1, offsets=None, split=False):
        return product(where, acts, acts_other, weight, other[group], group, block, picks, steps, offsets, split)

    down, up = make(
        place, 0, (2, 1), [lambda i, s: (0, lax.rem(s[1] + 4, Z)), lambda i, s: (0, lax.rem(s[1] + 3, Z))]
    )
    down, up = down[:, 0], up[:, 0]
    sent = make(after(place, down), 1, (1, Z), [lambda i, s: (1 - s[0], 0)], 1, [ORDER[k : k + 2] for k in (0, 2, 4, 6)])
    got = []

    down, up, piece = shift(down, -1), shift(up, 1), swap(sent[0], "yh")
    (full,) = make(after(place, sent[0]), 0, (1, Z), [lambda i, s: (i, 0)], 2, [ORDER], True)
    down, up, piece, full = join(down, up, piece, full)
    got.append(piece)
    down, up = add(down, full[2]), add(up, full[3])
    down, up, going = join(down, up, sent[1])

    here, near = after(place, down), after(near, down)
    down, up, piece = shift(down, -1), shift(up, 1), swap(going, "yh")
    (kept,) = make(here, 1, (1, Z), [lambda i, s: (s[0], 0)], 1, [ORDER])
    down, up, piece, kept = join(down, up, piece, kept)
    got.append(piece)
    down, up = add(down, full[4]), add(up, full[5])
    down, up, going = join(down, up, sent[2])

    near = after(near, down).reshape(2 * Z, -1, near.shape[-1])
    down, up, piece = shift(down, -1), shift(up, 1), swap(going, "yh")
    context = attend(place, queries, doc_ids, near, swap(near, "c"))
    down, up, piece, context = join(down, up, piece, context)
    got.append(piece)
    down = add(down, full[6])
    down, going, context = join(down, sent[3], context)

    residual = lax.all_to_all(context, EXP, split_axis=0, concat_axis=1, tiled=True)
    down, piece = shift(down, -1), swap(going, "yh")
    down, piece = join(down, piece)
    got.append(piece)
    first = add(down, up, full[7])

    def second_term(order):
        return kept[order], got[order // 2][order % 2]

    going = chunk_of(first, 1 - high)
    down, up = add(*second_term(0)), add(*second_term(1))
    down, up, going = join(down, up, going)
    down, up, moved = shift(down, -1), shift(up, 1), swap(going, "yh")
    down, up = join(down, up)
    down, up = add(down, *second_term(2)), add(up, *second_term(3))
    down, up = shift(down, -1), shift(up, 1)
    down, up, moved = join(down, up, moved)
    first = add(chunk_of(first, high), moved)
    down, up = add(down, *second_term(4)), add(up, *second_term(5))
    down, up = shift(down, -1), shift(up, 1)
    down, up = join(down, up)
    down = add(down, *second_term(6))
    second = add(shift(down, -1), up, *second_term(7))

    tokens = routes.shape[0]
    capacity = first.shape[0] // (2 * EXPERTS)
    mix = mixing(routes, route_weights, capacity)
    mixed = []
    for rows in (first, second):
        home = lax.all_to_all(
            rows.reshape(2 * EXPERTS, capacity, -1), ("c",) + EXP, split_axis=0, concat_axis=0, tiled=True
        )
        if rows is first:
            home = after(home, second)
        home = home.reshape(2, EXPERTS * capacity, -1)
        both = jnp.einsum("tr,crn->tcn", mix, home, preferred_element_type=jnp.float32)
        mixed.append(both[:tokens] + both[tokens:])
    mixed = jnp.concatenate(mixed, axis=2).reshape(tokens, -1)
    moe_out = residual.astype(jnp.float32) + mixed
    return (context, moe_out.astype(jnp.bfloat16))


def chunk_of(array, at):
    return lax.dynamic_index_in_dim(array, at, 0, keepdims=False)


def mixing(routes, route_weights, capacity):
    flat = routes.reshape(-1)
    pairs = jnp.arange(flat.shape[0])
    same = (flat[:, None] == flat[None, :]) & (pairs[None, :] < pairs[:, None])
    slot = jnp.sum(same.astype(jnp.int32), axis=1).reshape(routes.shape)
    row = routes * capacity + slot
    hit = row[:, :, None] == jnp.arange(EXPERTS * capacity)[None, None, :]
    mix = jnp.sum(jnp.where(hit, route_weights[:, :, None], 0.0), axis=1)
    coarse = mix.astype(jnp.bfloat16)
    fine = (mix - coarse.astype(jnp.float32)).astype(jnp.bfloat16)
    return jnp.concatenate([coarse, fine], axis=0)


def solution(mesh):
    inner = Mesh(mesh.devices.reshape(SHAPE), AXES)
    in_specs = (
        P(CTX, EXP),
        P(CTX, EXP, None),
        P(CTX),
        P(EXP, None, CTX),
        P(EXP, CTX, None),
        P(CTX + EXP, None),
        P(CTX + EXP, None),
    )
    out_specs = (P(CTX, EXP), P(CTX + EXP, None))
    return jax.shard_map(shards, mesh=inner, in_specs=in_specs, out_specs=out_specs, check_vma=False)
```

```python
import math

import jax
import jax.numpy as jnp
from jax import lax
from jax.experimental import pallas as pl
from jax.experimental.pallas import tpu as pltpu
from jax.sharding import Mesh
from jax.sharding import PartitionSpec as P

AXES = ("yh", "z", "c", "x", "yl")
SHAPE = (2, 8, 2, 4, 2)
CTX = ("yh", "z", "c")
EXP = ("x", "yl")
Z = 8
EXPERTS = 8
PAD = 16
GROUPS = 2
ORDER = (4, 3, 5, 2, 6, 1, 7, 0)
PRODUCT_VMEM = 16 * 1024 * 1024
ATTENTION_VMEM = 24 * 1024 * 1024


def shift(value, step):
    return lax.ppermute(value, "z", [(i, (i + step) % Z) for i in range(Z)])


def swap(value, axis):
    return lax.ppermute(value, axis, [(0, 1), (1, 0)])


def after(value, *earlier):
    return lax.optimization_barrier((value,) + earlier)[0]


def attention_kernel(head, place, q_ref, doc_ref, a_ref, b_ref, o_ref, q_all, scores, top, total, acc):
    tokens = q_ref.shape[0]
    groups = q_ref.shape[1] // head
    high, along, core = place[0], place[1], place[2]
    mine = (high * Z + along) * 2 + core
    for g in range(groups):
        q_all[g * tokens : (g + 1) * tokens, :] = q_ref[:, g * head : (g + 1) * head]
    row = doc_ref[...].astype(jnp.float32)
    query_docs = jnp.transpose(jnp.broadcast_to(row, (tokens, tokens)))
    query_pos = lax.broadcasted_iota(jnp.int32, (tokens, tokens), 0) + mine * tokens
    lane = lax.broadcasted_iota(jnp.int32, (tokens, tokens), 1)
    top[...] = jnp.full_like(top, -1e30)
    total[...] = jnp.zeros_like(total)
    acc[...] = jnp.zeros_like(acc)
    arrays = ((a_ref, 0), (b_ref, 1))

    def origin(k, other_core):
        other_high = lax.rem(k, 2)
        high_at = high + other_high - 2 * high * other_high
        core_at = core + other_core - 2 * core * other_core
        return (high_at * Z + lax.div(k, 2)) * 2 + core_at

    for n, (ref, other_core) in enumerate(arrays):

        def score(k, carry, ref=ref, n=n, other_core=other_core):
            where = origin(k, other_core)

            @pl.when(where <= mine)
            def _():
                docs = ref[k, tokens : tokens + PAD, :tokens].astype(jnp.float32)[:1]
                allowed = (docs == query_docs) & (where * tokens + lane <= query_pos)
                s = lax.dot_general(
                    q_all[...],
                    ref[k, :tokens, :head],
                    (((1,), (1,)), ((), ())),
                    preferred_element_type=jnp.float32,
                )
                s = s.reshape(groups, tokens, tokens)
                s = jnp.where(allowed[None], s, jnp.float32(-1e30)).reshape(groups * tokens, tokens)
                scores[n * 2 * Z + k] = s
                top[...] = jnp.maximum(top[...], s)

            return carry

        lax.fori_loop(0, 2 * Z, score, 0)
    top[...] = jnp.broadcast_to(jnp.max(top[...], axis=1, keepdims=True), top.shape)
    factor = math.log2(math.e) / math.sqrt(head)
    for n, (ref, other_core) in enumerate(arrays):

        def mix(k, carry, ref=ref, n=n, other_core=other_core):
            where = origin(k, other_core)

            @pl.when(where <= mine)
            def _():
                weights = jnp.exp2((scores[n * 2 * Z + k] - top[...]) * factor)
                total[...] += weights
                acc[...] += jnp.dot(
                    weights.astype(jnp.bfloat16),
                    ref[k, :tokens, head:],
                    preferred_element_type=jnp.float32,
                )

            return carry

        lax.fori_loop(0, 2 * Z, mix, 0)
    out = acc[...] / jnp.sum(total[...], axis=1, keepdims=True)
    out = out.astype(o_ref.dtype)
    for g in range(groups):
        o_ref[:, g * head : (g + 1) * head] = out[g * tokens : (g + 1) * tokens, :]


def key_block(keys_values, doc_ids):
    tokens, width = doc_ids.shape[0], keys_values.shape[2]
    docs = jnp.pad(doc_ids.astype(jnp.bfloat16)[None, :], ((0, PAD - 1), (0, width - tokens)))
    return jnp.concatenate([keys_values, docs[:, None, :]], axis=0)


def attend(place, queries, doc_ids, near, far):
    tokens, width = doc_ids.shape[0], near.shape[-1]
    head = width // 2
    rows = queries.shape[1] // head * tokens
    spec = pl.BlockSpec(memory_space=pltpu.VMEM)
    return pl.pallas_call(
        lambda *refs: attention_kernel(head, *refs),
        out_shape=jax.ShapeDtypeStruct(queries.shape, jnp.bfloat16),
        in_specs=[pl.BlockSpec(memory_space=pltpu.SMEM)] + [spec] * 4,
        out_specs=spec,
        scratch_shapes=[
            pltpu.VMEM((rows, head), jnp.bfloat16),
            pltpu.VMEM((4 * Z, rows, tokens), jnp.float32),
            pltpu.VMEM((rows, tokens), jnp.float32),
            pltpu.VMEM((rows, tokens), jnp.float32),
            pltpu.VMEM((rows, head), jnp.float32),
        ],
        compiler_params=pltpu.CompilerParams(vmem_limit_bytes=ATTENTION_VMEM),
        name="attention",
    )(place, queries, doc_ids[None, :], near, far)


def slice_kernel(place, *refs):
    for i in range(GROUPS):
        refs[GROUPS + i][...] = refs[i][...]


def other_columns(place, weight, columns):
    depth, strips = weight.shape[0], 4
    rows = depth // strips
    return pl.pallas_call(
        slice_kernel,
        out_shape=[jax.ShapeDtypeStruct((depth, columns), weight.dtype)] * GROUPS,
        grid_spec=pltpu.PrefetchScalarGridSpec(
            num_scalar_prefetch=1,
            grid=(strips,),
            in_specs=[
                pl.BlockSpec((rows, columns), lambda i, s, g=g: (i, (1 - s[2]) * GROUPS + g)) for g in range(GROUPS)
            ],
            out_specs=[pl.BlockSpec((rows, columns), lambda i, s: (i, 0))] * GROUPS,
        ),
        compiler_params=pltpu.CompilerParams(vmem_limit_bytes=PRODUCT_VMEM),
        name="columns",
    )(place, *([pltpu.with_memory_space_constraint(weight, pltpu.HBM)] * GROUPS))


def product_kernel(count, offsets, place, *refs):
    depth = refs[0].shape[-1]
    wa_ref, wb_ref = refs[2 * count : 2 * count + 2]
    a = jnp.concatenate([ref[...].reshape(-1, depth) for ref in refs[:count]], axis=0)
    b = jnp.concatenate([ref[...].reshape(-1, depth) for ref in refs[count : 2 * count]], axis=0)
    out = jnp.dot(a, wa_ref[...], preferred_element_type=jnp.float32)
    out += jnp.dot(b, wb_ref[...], preferred_element_type=jnp.float32)
    out = out.astype(jnp.bfloat16)
    if offsets is None:
        o_refs = refs[2 * count + 2 :]
        rows = out.shape[0] // len(o_refs)
        for i, o_ref in enumerate(o_refs):
            o_ref[...] = out[i * rows : (i + 1) * rows].reshape(o_ref.shape)
    else:
        o_refs, chunks = refs[2 * count + 2 : -1], refs[-1]
        chunks[...] = out.reshape(chunks.shape)
        for o_ref, picks in zip(o_refs, offsets):
            for k, offset in enumerate(picks):
                o_ref[k] = chunks[lax.rem(place[1] + offset, Z)].reshape(o_ref.shape[1:])


def product(place, acts, acts_other, weight, other, first, block, picks, steps, offsets, split):
    depth, rows = acts.shape[-1], acts.shape[2]
    columns = other.shape[1]
    tile = columns // 2
    half, start = weight.shape[1] // (2 * tile), first * 2
    specs = [pl.BlockSpec(block + (rows, depth), lambda j, i, s, pick=pick: pick(i, s) + (0, 0)) for pick in picks]
    if offsets is None:
        shapes, blocks = [block + (rows, columns)] * len(picks), [block + (rows, tile)] * len(picks)
        scratch = []
    else:
        split = (steps,) if split else ()
        shapes = [(len(o),) + split + (rows, columns) for o in offsets]
        blocks = [(len(o),) + (1,) * len(split) + (rows, tile) for o in offsets]
        scratch = [pltpu.VMEM(block[1:] + (rows, tile), jnp.bfloat16)]

    def out_map(rank):
        if rank == 3:
            return lambda j, i, s: (0, 0, j)
        return lambda j, i, s: (0, i, 0, j)

    weight = pltpu.with_memory_space_constraint(weight, pltpu.HBM)
    return pl.pallas_call(
        lambda *refs: product_kernel(len(picks), offsets, *refs),
        out_shape=[jax.ShapeDtypeStruct(shape, jnp.bfloat16) for shape in shapes],
        grid_spec=pltpu.PrefetchScalarGridSpec(
            num_scalar_prefetch=1,
            grid=(2, steps),
            in_specs=specs
            + specs
            + [
                pl.BlockSpec((depth, tile), lambda j, i, s: (0, s[2] * half + start + j)),
                pl.BlockSpec((depth, tile), lambda j, i, s: (0, j)),
            ],
            out_specs=[pl.BlockSpec(b, out_map(len(b))) for b in blocks],
            scratch_shapes=scratch,
        ),
        compiler_params=pltpu.CompilerParams(vmem_limit_bytes=PRODUCT_VMEM),
        name="product",
    )(place, *([acts] * len(picks)), *([acts_other] * len(picks)), weight, other)


def add(*terms):
    total = terms[0].astype(jnp.float32)
    for term in terms[1:]:
        total = total + term.astype(jnp.float32)
    return total.astype(jnp.bfloat16)


def join(*values):
    return lax.optimization_barrier(values)


def shards(queries, keys_values, doc_ids, gate_up, down_weight, routes, route_weights):
    high, along, core = (lax.axis_index(name).astype(jnp.int32) for name in CTX)
    place = jnp.stack([high, along, core])
    weight = down_weight[0]
    columns = weight.shape[1] // (2 * GROUPS)
    depth = weight.shape[0]
    acts = gate_up[0].reshape(2, Z, -1, depth)

    acts_other = swap(gate_up[0], "c")
    parts = other_columns(place, weight, columns)
    other = [swap(part, "c") for part in parts]
    block = key_block(keys_values, after(doc_ids, *parts))
    block_other = swap(block, "yh")
    acts_other, other[0], block_other = join(acts_other, other[0], block_other)
    acts_other = acts_other.reshape(2, Z, -1, depth)
    pair = jnp.concatenate([block, block_other], axis=0)
    near = lax.all_gather(pair, "z", axis=0, tiled=True)

    def make(where, group, block, picks, steps=1, offsets=None, split=False):
        return product(where, acts, acts_other, weight, other[group], group, block, picks, steps, offsets, split)

    def first_terms(where, orders):
        picks = [lambda i, s, k=ORDER[order]: (0, lax.rem(s[1] + k, Z)) for order in orders]
        return [term[:, 0] for term in make(where, 0, (2, 1), picks)]

    down, up = first_terms(after(place, pair), (0, 1))
    sent = make(after(place, down), 1, (1, Z), [lambda i, s: (1 - s[0], 0)], 1, [ORDER[k : k + 2] for k in (0, 2, 4, 6)])
    got = []

    down, up, piece = shift(down, -1), shift(up, 1), swap(sent[0], "yh")
    down_term, up_term = first_terms(after(place, sent[0]), (2, 3))
    down, up, piece, down_term, up_term = join(down, up, piece, down_term, up_term)
    got.append(piece)
    down, up = add(down, down_term), add(up, up_term)
    down, up, going = join(down, up, sent[1])

    here = after(place, down)
    down, up, piece = shift(down, -1), shift(up, 1), swap(going, "yh")
    (kept,) = make(here, 1, (1, Z), [lambda i, s: (s[0], 0)], 1, [ORDER])
    terms = first_terms(after(place, kept), (4, 5, 6, 7))
    down, up, piece, *terms = join(down, up, piece, *terms)
    got.append(piece)
    down, up = add(down, terms[0]), add(up, terms[1])
    down, up, going = join(down, up, sent[2])

    down, up, piece = shift(down, -1), shift(up, 1), swap(going, "yh")
    down, up, piece, near = join(down, up, piece, near)
    got.append(piece)
    down = add(down, terms[2])
    down, going, near = join(down, sent[3], near)

    near = near.reshape(2 * Z, -1, near.shape[-1])
    down, last = shift(down, -1), swap(going, "yh")
    context = attend(place, queries, doc_ids, near, swap(near, "c"))
    down, context = join(down, context)
    first = add(down, up, terms[3])

    def second_term(order):
        return kept[order], got[order // 2][order % 2]

    going = chunk_of(first, 1 - high)
    down, up = add(*second_term(0)), add(*second_term(1))
    down, up, going = join(down, up, going)
    down, up, moved = shift(down, -1), shift(up, 1), swap(going, "yh")
    residual = lax.all_to_all(context, EXP, split_axis=0, concat_axis=1, tiled=True)
    down, up = join(down, up)
    down, up = add(down, *second_term(2)), add(up, *second_term(3))
    down, up = shift(down, -1), shift(up, 1)
    down, up, moved, last = join(down, up, moved, last)
    got.append(last)
    first = add(chunk_of(first, high), moved)
    down, up = add(down, *second_term(4)), add(up, *second_term(5))
    down, up = shift(down, -1), shift(up, 1)
    down, up = join(down, up)
    down = add(down, *second_term(6))
    down, residual = join(shift(down, -1), residual)
    second = add(down, up, *second_term(7))

    tokens = routes.shape[0]
    capacity = first.shape[0] // (2 * EXPERTS)
    mix = mixing(routes, route_weights, capacity)
    rows = jnp.concatenate([first, second], axis=1).reshape(2 * EXPERTS, capacity, -1)
    home = lax.all_to_all(rows, ("c",) + EXP, split_axis=0, concat_axis=0, tiled=True)
    home = home.reshape(2, EXPERTS * capacity, -1)
    both = jnp.einsum("tr,crn->tcn", mix, home, preferred_element_type=jnp.float32)
    mixed = (both[:tokens] + both[tokens:]).reshape(tokens, -1)
    moe_out = residual.astype(jnp.float32) + mixed
    return (context, moe_out.astype(jnp.bfloat16))


def chunk_of(array, at):
    return lax.dynamic_index_in_dim(array, at, 0, keepdims=False)


def mixing(routes, route_weights, capacity):
    flat = routes.reshape(-1)
    pairs = jnp.arange(flat.shape[0])
    same = (flat[:, None] == flat[None, :]) & (pairs[None, :] < pairs[:, None])
    slot = jnp.sum(same.astype(jnp.int32), axis=1).reshape(routes.shape)
    row = routes * capacity + slot
    hit = row[:, :, None] == jnp.arange(EXPERTS * capacity)[None, None, :]
    mix = jnp.sum(jnp.where(hit, route_weights[:, :, None], 0.0), axis=1)
    coarse = mix.astype(jnp.bfloat16)
    fine = (mix - coarse.astype(jnp.float32)).astype(jnp.bfloat16)
    return jnp.concatenate([coarse, fine], axis=0)


def solution(mesh):
    inner = Mesh(mesh.devices.reshape(SHAPE), AXES)
    in_specs = (
        P(CTX, EXP),
        P(CTX, EXP, None),
        P(CTX),
        P(EXP, None, CTX),
        P(EXP, CTX, None),
        P(CTX + EXP, None),
        P(CTX + EXP, None),
    )
    out_specs = (P(CTX, EXP), P(CTX + EXP, None))
    return jax.shard_map(shards, mesh=inner, in_specs=in_specs, out_specs=out_specs, check_vma=False)
```

```python
import math

import jax
import jax.numpy as jnp
from jax import lax
from jax.experimental import pallas as pl
from jax.experimental.pallas import tpu as pltpu
from jax.sharding import Mesh
from jax.sharding import PartitionSpec as P

AXES = ("yh", "z", "c", "x", "yl")
SHAPE = (2, 8, 2, 4, 2)
CTX = ("yh", "z", "c")
EXP = ("x", "yl")
Z = 8
EXPERTS = 8
PAD = 16
GROUPS = 2
ORDER = (4, 3, 5, 2, 6, 1, 7, 0)
PRODUCT_VMEM = 16 * 1024 * 1024
ATTENTION_VMEM = 24 * 1024 * 1024


def shift(value, step):
    return lax.ppermute(value, "z", [(i, (i + step) % Z) for i in range(Z)])


def swap(value, axis):
    return lax.ppermute(value, axis, [(0, 1), (1, 0)])


def after(value, *earlier):
    return lax.optimization_barrier((value,) + earlier)[0]


def attention_kernel(head, place, q_ref, doc_ref, a_ref, b_ref, o_ref, q_all, scores, top, total, acc):
    tokens = q_ref.shape[0]
    groups = q_ref.shape[1] // head
    high, along, core = place[0], place[1], place[2]
    mine = (high * Z + along) * 2 + core
    for g in range(groups):
        q_all[g * tokens : (g + 1) * tokens, :] = q_ref[:, g * head : (g + 1) * head]
    row = doc_ref[...].astype(jnp.float32)
    query_docs = jnp.transpose(jnp.broadcast_to(row, (tokens, tokens)))
    query_pos = lax.broadcasted_iota(jnp.int32, (tokens, tokens), 0) + mine * tokens
    lane = lax.broadcasted_iota(jnp.int32, (tokens, tokens), 1)
    top[...] = jnp.full_like(top, -1e30)
    total[...] = jnp.zeros_like(total)
    acc[...] = jnp.zeros_like(acc)
    arrays = ((a_ref, 0), (b_ref, 1))

    def origin(k, other_core):
        other_high = lax.rem(k, 2)
        high_at = high + other_high - 2 * high * other_high
        core_at = core + other_core - 2 * core * other_core
        return (high_at * Z + lax.div(k, 2)) * 2 + core_at

    for n, (ref, other_core) in enumerate(arrays):

        def score(k, carry, ref=ref, n=n, other_core=other_core):
            where = origin(k, other_core)

            @pl.when(where <= mine)
            def _():
                docs = ref[k, tokens : tokens + PAD, :tokens].astype(jnp.float32)[:1]
                allowed = (docs == query_docs) & (where * tokens + lane <= query_pos)
                s = lax.dot_general(
                    q_all[...],
                    ref[k, :tokens, :head],
                    (((1,), (1,)), ((), ())),
                    preferred_element_type=jnp.float32,
                )
                s = s.reshape(groups, tokens, tokens)
                s = jnp.where(allowed[None], s, jnp.float32(-1e30)).reshape(groups * tokens, tokens)
                scores[n * 2 * Z + k] = s
                top[...] = jnp.maximum(top[...], s)

            return carry

        lax.fori_loop(0, 2 * Z, score, 0)
    top[...] = jnp.broadcast_to(jnp.max(top[...], axis=1, keepdims=True), top.shape)
    factor = math.log2(math.e) / math.sqrt(head)
    for n, (ref, other_core) in enumerate(arrays):

        def mix(k, carry, ref=ref, n=n, other_core=other_core):
            where = origin(k, other_core)

            @pl.when(where <= mine)
            def _():
                weights = jnp.exp2((scores[n * 2 * Z + k] - top[...]) * factor)
                total[...] += weights
                acc[...] += jnp.dot(
                    weights.astype(jnp.bfloat16),
                    ref[k, :tokens, head:],
                    preferred_element_type=jnp.float32,
                )

            return carry

        lax.fori_loop(0, 2 * Z, mix, 0)
    out = acc[...] / jnp.sum(total[...], axis=1, keepdims=True)
    out = out.astype(o_ref.dtype)
    for g in range(groups):
        o_ref[:, g * head : (g + 1) * head] = out[g * tokens : (g + 1) * tokens, :]


def key_block(keys_values, doc_ids):
    tokens, width = doc_ids.shape[0], keys_values.shape[2]
    docs = jnp.pad(doc_ids.astype(jnp.bfloat16)[None, :], ((0, PAD - 1), (0, width - tokens)))
    return jnp.concatenate([keys_values, docs[:, None, :]], axis=0)


def attend(place, queries, doc_ids, near, far):
    tokens, width = doc_ids.shape[0], near.shape[-1]
    head = width // 2
    rows = queries.shape[1] // head * tokens
    spec = pl.BlockSpec(memory_space=pltpu.VMEM)
    return pl.pallas_call(
        lambda *refs: attention_kernel(head, *refs),
        out_shape=jax.ShapeDtypeStruct(queries.shape, jnp.bfloat16),
        in_specs=[pl.BlockSpec(memory_space=pltpu.SMEM)] + [spec] * 4,
        out_specs=spec,
        scratch_shapes=[
            pltpu.VMEM((rows, head), jnp.bfloat16),
            pltpu.VMEM((4 * Z, rows, tokens), jnp.float32),
            pltpu.VMEM((rows, tokens), jnp.float32),
            pltpu.VMEM((rows, tokens), jnp.float32),
            pltpu.VMEM((rows, head), jnp.float32),
        ],
        compiler_params=pltpu.CompilerParams(vmem_limit_bytes=ATTENTION_VMEM),
        name="attention",
    )(place, queries, doc_ids[None, :], near, far)


def slice_kernel(place, w_ref, o_ref):
    o_ref[...] = w_ref[...]


def other_columns(place, weight, columns, group):
    depth, strips = weight.shape[0], 4
    rows = depth // strips
    return pl.pallas_call(
        slice_kernel,
        out_shape=jax.ShapeDtypeStruct((depth, columns), weight.dtype),
        grid_spec=pltpu.PrefetchScalarGridSpec(
            num_scalar_prefetch=1,
            grid=(strips,),
            in_specs=[pl.BlockSpec((rows, columns), lambda i, s: (i, (1 - s[2]) * GROUPS + group))],
            out_specs=pl.BlockSpec((rows, columns), lambda i, s: (i, 0)),
        ),
        compiler_params=pltpu.CompilerParams(vmem_limit_bytes=PRODUCT_VMEM),
        name="columns",
    )(place, pltpu.with_memory_space_constraint(weight, pltpu.HBM))


def product_kernel(count, offsets, place, *refs):
    depth = refs[0].shape[-1]
    wa_ref, wb_ref = refs[2 * count : 2 * count + 2]
    a = jnp.concatenate([ref[...].reshape(-1, depth) for ref in refs[:count]], axis=0)
    b = jnp.concatenate([ref[...].reshape(-1, depth) for ref in refs[count : 2 * count]], axis=0)
    out = jnp.dot(a, wa_ref[...], preferred_element_type=jnp.float32)
    out += jnp.dot(b, wb_ref[...], preferred_element_type=jnp.float32)
    out = out.astype(jnp.bfloat16)
    if offsets is None:
        o_refs = refs[2 * count + 2 :]
        rows = out.shape[0] // len(o_refs)
        for i, o_ref in enumerate(o_refs):
            o_ref[...] = out[i * rows : (i + 1) * rows].reshape(o_ref.shape)
    else:
        o_refs, chunks = refs[2 * count + 2 : -1], refs[-1]
        chunks[...] = out.reshape(chunks.shape)
        for o_ref, picks in zip(o_refs, offsets):
            for k, offset in enumerate(picks):
                o_ref[k] = chunks[lax.rem(place[1] + offset, Z)].reshape(o_ref.shape[1:])


def product(place, acts, acts_other, weight, other, first, block, picks, steps, offsets, split):
    depth, rows = acts.shape[-1], acts.shape[2]
    columns = other.shape[1]
    tile = columns // 2
    half, start = weight.shape[1] // (2 * tile), first * 2
    specs = [pl.BlockSpec(block + (rows, depth), lambda j, i, s, pick=pick: pick(i, s) + (0, 0)) for pick in picks]
    if offsets is None:
        shapes, blocks = [block + (rows, columns)] * len(picks), [block + (rows, tile)] * len(picks)
        scratch = []
    else:
        split = (steps,) if split else ()
        shapes = [(len(o),) + split + (rows, columns) for o in offsets]
        blocks = [(len(o),) + (1,) * len(split) + (rows, tile) for o in offsets]
        scratch = [pltpu.VMEM(block[1:] + (rows, tile), jnp.bfloat16)]

    def out_map(rank):
        if rank == 3:
            return lambda j, i, s: (0, 0, j)
        return lambda j, i, s: (0, i, 0, j)

    weight = pltpu.with_memory_space_constraint(weight, pltpu.HBM)
    return pl.pallas_call(
        lambda *refs: product_kernel(len(picks), offsets, *refs),
        out_shape=[jax.ShapeDtypeStruct(shape, jnp.bfloat16) for shape in shapes],
        grid_spec=pltpu.PrefetchScalarGridSpec(
            num_scalar_prefetch=1,
            grid=(2, steps),
            in_specs=specs
            + specs
            + [
                pl.BlockSpec((depth, tile), lambda j, i, s: (0, s[2] * half + start + j)),
                pl.BlockSpec((depth, tile), lambda j, i, s: (0, j)),
            ],
            out_specs=[pl.BlockSpec(b, out_map(len(b))) for b in blocks],
            scratch_shapes=scratch,
        ),
        compiler_params=pltpu.CompilerParams(vmem_limit_bytes=PRODUCT_VMEM),
        name="product",
    )(place, *([acts] * len(picks)), *([acts_other] * len(picks)), weight, other)


def add(*terms):
    total = terms[0].astype(jnp.float32)
    for term in terms[1:]:
        total = total + term.astype(jnp.float32)
    return total.astype(jnp.bfloat16)


def join(*values):
    return lax.optimization_barrier(values)


def shards(queries, keys_values, doc_ids, gate_up, down_weight, routes, route_weights):
    high, along, core = (lax.axis_index(name).astype(jnp.int32) for name in CTX)
    place = jnp.stack([high, along, core])
    weight = down_weight[0]
    columns = weight.shape[1] // (2 * GROUPS)
    depth = weight.shape[0]
    acts = gate_up[0].reshape(2, Z, -1, depth)

    acts_other = swap(gate_up[0], "c")
    part = other_columns(place, weight, columns, 0)
    other = [swap(part, "c")]
    part = other_columns(after(place, part), weight, columns, 1)
    acts_other, other[0], part = join(acts_other, other[0], part)
    other.append(swap(part, "c"))
    acts_other = acts_other.reshape(2, Z, -1, depth)

    def make(where, group, block, picks, offsets=None):
        return product(where, acts, acts_other, weight, other[group], group, block, picks, 1, offsets, False)

    def first_terms(where, orders):
        picks = [lambda i, s, k=ORDER[order]: (0, lax.rem(s[1] + k, Z)) for order in orders]
        return [term[:, 0] for term in make(where, 0, (2, 1), picks)]

    down, up = first_terms(place, (0, 1))
    block = key_block(keys_values, after(doc_ids, down))
    pair = jnp.concatenate([block, swap(block, "yh")], axis=0)
    near = lax.all_gather(pair, "z", axis=0, tiled=True)
    here = after(place, block)
    down, up = shift(down, -1), shift(up, 1)
    down_term, up_term = first_terms(here, (2, 3))
    sent = make(
        after(place, down_term), 1, (1, Z), [lambda i, s: (1 - s[0], 0)], [ORDER[k : k + 2] for k in (0, 2, 4, 6)]
    )
    down, up, down_term, up_term, pair, *sent = join(down, up, down_term, up_term, pair, *sent)
    down, up = add(down, down_term), add(up, up_term)
    down, up, sent[0] = join(down, up, sent[0])

    here = after(place, down)
    down, up = shift(down, -1), shift(up, 1)
    got = [swap(sent[0], "yh")]
    terms = first_terms(here, (4, 5, 6, 7))
    down, up, *terms = join(down, up, *terms)
    down, up = add(down, terms[0]), add(up, terms[1])
    down, up, sent[1] = join(down, up, sent[1])

    here = after(place, down)
    down, up = shift(down, -1), shift(up, 1)
    got.append(swap(after(sent[1], got[0]), "yh"))
    (kept,) = make(here, 1, (1, Z), [lambda i, s: (s[0], 0)], [ORDER])
    down, up, near, kept, got[0] = join(down, up, near, kept, got[0])
    down = add(down, terms[2])
    down, sent[2], near = join(down, sent[2], near)

    near = near.reshape(2 * Z, -1, near.shape[-1])
    down = shift(down, -1)
    got.append(swap(after(sent[2], got[1]), "yh"))
    context = attend(place, queries, doc_ids, near, swap(near, "c"))
    down, context, got[1] = join(down, context, got[1])
    first = add(down, up, terms[3])

    def second_term(order):
        return kept[order], got[order // 2][order % 2]

    going = chunk_of(first, 1 - high)
    down, up = add(*second_term(0)), add(*second_term(1))
    down, up, going, sent[3] = join(down, up, going, sent[3])
    down, up = shift(down, -1), shift(up, 1)
    got.append(swap(after(sent[3], got[2]), "yh"))
    residual = lax.all_to_all(context, EXP, split_axis=0, concat_axis=1, tiled=True)
    down, up, got[2] = join(down, up, got[2])
    down, up = add(down, *second_term(2)), add(up, *second_term(3))
    down, up, going = join(down, up, going)
    down, up, moved = shift(down, -1), shift(up, 1), swap(after(going, got[3]), "yh")
    down, up, got[3] = join(down, up, got[3])
    down, up = add(down, *second_term(4)), add(up, *second_term(5))
    down, up = join(down, up)
    down, up = shift(down, -1), shift(up, 1)
    down, up, moved = join(down, up, moved)
    down = add(down, *second_term(6))
    first = add(chunk_of(first, high), moved)
    down, residual = join(shift(down, -1), residual)
    second = add(down, up, *second_term(7))

    tokens = routes.shape[0]
    capacity = first.shape[0] // (2 * EXPERTS)
    mix = mixing(routes, route_weights, capacity)
    rows = jnp.concatenate([first, second], axis=1).reshape(2 * EXPERTS, capacity, -1)
    home = lax.all_to_all(rows, ("c",) + EXP, split_axis=0, concat_axis=0, tiled=True)
    home = home.reshape(2, EXPERTS * capacity, -1)
    both = jnp.einsum("tr,crn->tcn", mix, home, preferred_element_type=jnp.float32)
    mixed = (both[:tokens] + both[tokens:]).reshape(tokens, -1)
    moe_out = residual.astype(jnp.float32) + mixed
    return (context, moe_out.astype(jnp.bfloat16))


def chunk_of(array, at):
    return lax.dynamic_index_in_dim(array, at, 0, keepdims=False)


def mixing(routes, route_weights, capacity):
    flat = routes.reshape(-1)
    pairs = jnp.arange(flat.shape[0])
    same = (flat[:, None] == flat[None, :]) & (pairs[None, :] < pairs[:, None])
    slot = jnp.sum(same.astype(jnp.int32), axis=1).reshape(routes.shape)
    row = routes * capacity + slot
    hit = row[:, :, None] == jnp.arange(EXPERTS * capacity)[None, None, :]
    mix = jnp.sum(jnp.where(hit, route_weights[:, :, None], 0.0), axis=1)
    coarse = mix.astype(jnp.bfloat16)
    fine = (mix - coarse.astype(jnp.float32)).astype(jnp.bfloat16)
    return jnp.concatenate([coarse, fine], axis=0)


def solution(mesh):
    inner = Mesh(mesh.devices.reshape(SHAPE), AXES)
    in_specs = (
        P(CTX, EXP),
        P(CTX, EXP, None),
        P(CTX),
        P(EXP, None, CTX),
        P(EXP, CTX, None),
        P(CTX + EXP, None),
        P(CTX + EXP, None),
    )
    out_specs = (P(CTX, EXP), P(CTX + EXP, None))
    return jax.shard_map(shards, mesh=inner, in_specs=in_specs, out_specs=out_specs, check_vma=False)
```

```python
import math

import jax
import jax.numpy as jnp
from jax import lax
from jax.experimental import pallas as pl
from jax.experimental.pallas import tpu as pltpu
from jax.sharding import Mesh
from jax.sharding import PartitionSpec as P

AXES = ("yh", "z", "c", "x", "yl")
SHAPE = (2, 8, 2, 4, 2)
CTX = ("yh", "z", "c")
EXP = ("x", "yl")
Z = 8
EXPERTS = 8
PAD = 16
GROUPS = 2
ORDER = (4, 3, 5, 2, 6, 1, 7, 0)
PRODUCT_VMEM = 16 * 1024 * 1024
ATTENTION_VMEM = 24 * 1024 * 1024


def shift(value, step):
    return lax.ppermute(value, "z", [(i, (i + step) % Z) for i in range(Z)])


def swap(value, axis):
    return lax.ppermute(value, axis, [(0, 1), (1, 0)])


def after(value, *earlier):
    return lax.optimization_barrier((value,) + earlier)[0]


def attention_kernel(head, place, q_ref, doc_ref, a_ref, b_ref, o_ref, q_all, scores, top, total, acc):
    tokens = q_ref.shape[0]
    groups = q_ref.shape[1] // head
    high, along, core = place[0], place[1], place[2]
    mine = (high * Z + along) * 2 + core
    for g in range(groups):
        q_all[g * tokens : (g + 1) * tokens, :] = q_ref[:, g * head : (g + 1) * head]
    row = doc_ref[...].astype(jnp.float32)
    query_docs = jnp.transpose(jnp.broadcast_to(row, (tokens, tokens)))
    query_pos = lax.broadcasted_iota(jnp.int32, (tokens, tokens), 0) + mine * tokens
    lane = lax.broadcasted_iota(jnp.int32, (tokens, tokens), 1)
    top[...] = jnp.full_like(top, -1e30)
    total[...] = jnp.zeros_like(total)
    acc[...] = jnp.zeros_like(acc)
    arrays = ((a_ref, 0), (b_ref, 1))

    def origin(k, other_core):
        other_high = lax.rem(k, 2)
        high_at = high + other_high - 2 * high * other_high
        core_at = core + other_core - 2 * core * other_core
        return (high_at * Z + lax.div(k, 2)) * 2 + core_at

    for n, (ref, other_core) in enumerate(arrays):

        def score(k, carry, ref=ref, n=n, other_core=other_core):
            where = origin(k, other_core)

            @pl.when(where <= mine)
            def _():
                docs = ref[k, tokens : tokens + PAD, :tokens].astype(jnp.float32)[:1]
                allowed = (docs == query_docs) & (where * tokens + lane <= query_pos)
                s = lax.dot_general(
                    q_all[...],
                    ref[k, :tokens, :head],
                    (((1,), (1,)), ((), ())),
                    preferred_element_type=jnp.float32,
                )
                s = s.reshape(groups, tokens, tokens)
                s = jnp.where(allowed[None], s, jnp.float32(-1e30)).reshape(groups * tokens, tokens)
                scores[n * 2 * Z + k] = s
                top[...] = jnp.maximum(top[...], s)

            return carry

        lax.fori_loop(0, 2 * Z, score, 0)
    top[...] = jnp.broadcast_to(jnp.max(top[...], axis=1, keepdims=True), top.shape)
    factor = math.log2(math.e) / math.sqrt(head)
    for n, (ref, other_core) in enumerate(arrays):

        def mix(k, carry, ref=ref, n=n, other_core=other_core):
            where = origin(k, other_core)

            @pl.when(where <= mine)
            def _():
                weights = jnp.exp2((scores[n * 2 * Z + k] - top[...]) * factor)
                total[...] += weights
                acc[...] += jnp.dot(
                    weights.astype(jnp.bfloat16),
                    ref[k, :tokens, head:],
                    preferred_element_type=jnp.float32,
                )

            return carry

        lax.fori_loop(0, 2 * Z, mix, 0)
    out = acc[...] / jnp.sum(total[...], axis=1, keepdims=True)
    out = out.astype(o_ref.dtype)
    for g in range(groups):
        o_ref[:, g * head : (g + 1) * head] = out[g * tokens : (g + 1) * tokens, :]


def key_block(keys_values, doc_ids):
    tokens, width = doc_ids.shape[0], keys_values.shape[2]
    docs = jnp.pad(doc_ids.astype(jnp.bfloat16)[None, :], ((0, PAD - 1), (0, width - tokens)))
    return jnp.concatenate([keys_values, docs[:, None, :]], axis=0)


def attend(place, queries, doc_ids, near, far):
    tokens, width = doc_ids.shape[0], near.shape[-1]
    head = width // 2
    rows = queries.shape[1] // head * tokens
    spec = pl.BlockSpec(memory_space=pltpu.VMEM)
    return pl.pallas_call(
        lambda *refs: attention_kernel(head, *refs),
        out_shape=jax.ShapeDtypeStruct(queries.shape, jnp.bfloat16),
        in_specs=[pl.BlockSpec(memory_space=pltpu.SMEM)] + [spec] * 4,
        out_specs=spec,
        scratch_shapes=[
            pltpu.VMEM((rows, head), jnp.bfloat16),
            pltpu.VMEM((4 * Z, rows, tokens), jnp.float32),
            pltpu.VMEM((rows, tokens), jnp.float32),
            pltpu.VMEM((rows, tokens), jnp.float32),
            pltpu.VMEM((rows, head), jnp.float32),
        ],
        compiler_params=pltpu.CompilerParams(vmem_limit_bytes=ATTENTION_VMEM),
        name="attention",
    )(place, queries, doc_ids[None, :], near, far)


def slice_kernel(place, w_ref, o_ref):
    o_ref[...] = w_ref[...]


def other_columns(place, weight, columns, group):
    depth, strips = weight.shape[0], 4
    rows = depth // strips
    return pl.pallas_call(
        slice_kernel,
        out_shape=jax.ShapeDtypeStruct((depth, columns), weight.dtype),
        grid_spec=pltpu.PrefetchScalarGridSpec(
            num_scalar_prefetch=1,
            grid=(strips,),
            in_specs=[pl.BlockSpec((rows, columns), lambda i, s: (i, (1 - s[2]) * GROUPS + group))],
            out_specs=pl.BlockSpec((rows, columns), lambda i, s: (i, 0)),
        ),
        compiler_params=pltpu.CompilerParams(vmem_limit_bytes=PRODUCT_VMEM),
        name="columns",
    )(place, pltpu.with_memory_space_constraint(weight, pltpu.HBM))


def product_kernel(count, offsets, place, *refs):
    depth = refs[0].shape[-1]
    wa_ref, wb_ref = refs[2 * count : 2 * count + 2]
    a = jnp.concatenate([ref[...].reshape(-1, depth) for ref in refs[:count]], axis=0)
    b = jnp.concatenate([ref[...].reshape(-1, depth) for ref in refs[count : 2 * count]], axis=0)
    out = jnp.dot(a, wa_ref[...], preferred_element_type=jnp.float32)
    out += jnp.dot(b, wb_ref[...], preferred_element_type=jnp.float32)
    out = out.astype(jnp.bfloat16)
    if offsets is None:
        o_refs = refs[2 * count + 2 :]
        rows = out.shape[0] // len(o_refs)
        for i, o_ref in enumerate(o_refs):
            o_ref[...] = out[i * rows : (i + 1) * rows].reshape(o_ref.shape)
    else:
        o_refs, chunks = refs[2 * count + 2 : -1], refs[-1]
        chunks[...] = out.reshape(chunks.shape)
        for o_ref, picks in zip(o_refs, offsets):
            for k, offset in enumerate(picks):
                o_ref[k] = chunks[lax.rem(place[1] + offset, Z)].reshape(o_ref.shape[1:])


def product(place, acts, acts_other, weight, other, first, block, picks, steps, offsets, split):
    depth, rows = acts.shape[-1], acts.shape[2]
    columns = other.shape[1]
    tile = columns // 2
    half, start = weight.shape[1] // (2 * tile), first * 2
    specs = [pl.BlockSpec(block + (rows, depth), lambda j, i, s, pick=pick: pick(i, s) + (0, 0)) for pick in picks]
    if offsets is None:
        shapes, blocks = [block + (rows, columns)] * len(picks), [block + (rows, tile)] * len(picks)
        scratch = []
    else:
        split = (steps,) if split else ()
        shapes = [(len(o),) + split + (rows, columns) for o in offsets]
        blocks = [(len(o),) + (1,) * len(split) + (rows, tile) for o in offsets]
        scratch = [pltpu.VMEM(block[1:] + (rows, tile), jnp.bfloat16)]

    def out_map(rank):
        if rank == 3:
            return lambda j, i, s: (0, 0, j)
        return lambda j, i, s: (0, i, 0, j)

    weight = pltpu.with_memory_space_constraint(weight, pltpu.HBM)
    return pl.pallas_call(
        lambda *refs: product_kernel(len(picks), offsets, *refs),
        out_shape=[jax.ShapeDtypeStruct(shape, jnp.bfloat16) for shape in shapes],
        grid_spec=pltpu.PrefetchScalarGridSpec(
            num_scalar_prefetch=1,
            grid=(2, steps),
            in_specs=specs
            + specs
            + [
                pl.BlockSpec((depth, tile), lambda j, i, s: (0, s[2] * half + start + j)),
                pl.BlockSpec((depth, tile), lambda j, i, s: (0, j)),
            ],
            out_specs=[pl.BlockSpec(b, out_map(len(b))) for b in blocks],
            scratch_shapes=scratch,
        ),
        compiler_params=pltpu.CompilerParams(vmem_limit_bytes=PRODUCT_VMEM),
        name="product",
    )(place, *([acts] * len(picks)), *([acts_other] * len(picks)), weight, other)


def add(*terms):
    total = terms[0].astype(jnp.float32)
    for term in terms[1:]:
        total = total + term.astype(jnp.float32)
    return total.astype(jnp.bfloat16)


def join(*values):
    return lax.optimization_barrier(values)


def shards(queries, keys_values, doc_ids, gate_up, down_weight, routes, route_weights):
    high, along, core = (lax.axis_index(name).astype(jnp.int32) for name in CTX)
    place = jnp.stack([high, along, core])
    weight = down_weight[0]
    columns = weight.shape[1] // (2 * GROUPS)
    depth = weight.shape[0]
    acts = gate_up[0].reshape(2, Z, -1, depth)

    acts_other = swap(gate_up[0], "c")
    part = other_columns(place, weight, columns, 0)
    other = [swap(part, "c")]
    part = other_columns(after(place, part), weight, columns, 1)
    acts_other, other[0], part = join(acts_other, other[0], part)
    other.append(swap(part, "c"))
    acts_other = acts_other.reshape(2, Z, -1, depth)

    def make(where, group, block, picks, offsets=None):
        return product(where, acts, acts_other, weight, other[group], group, block, picks, 1, offsets, False)

    def first_terms(where, orders):
        picks = [lambda i, s, k=ORDER[order]: (0, lax.rem(s[1] + k, Z)) for order in orders]
        return [term[:, 0] for term in make(where, 0, (2, 1), picks)]

    down, up = first_terms(place, (0, 1))
    block = key_block(keys_values, after(doc_ids, down))
    pair = jnp.concatenate([block, swap(block, "yh")], axis=0)
    near = lax.all_gather(pair, "z", axis=0, tiled=True)
    here = after(place, block)
    down, up = shift(down, -1), shift(up, 1)
    down_term, up_term = first_terms(here, (2, 3))
    down, up, down_term, up_term, pair = join(down, up, down_term, up_term, pair)
    down, up = add(down, down_term), add(up, up_term)
    down, up = join(down, up)

    here = after(place, down)
    down, up = shift(down, -1), shift(up, 1)
    sent = list(make(here, 1, (1, Z), [lambda i, s: (1 - s[0], 0)], [ORDER[k : k + 2] for k in (0, 2, 4, 6)]))
    got = [swap(sent[0], "yh")]
    terms = first_terms(after(place, sent[0]), (4, 5, 6, 7))
    down, up, got[0], *terms = join(down, up, got[0], *terms)
    down, up = add(down, terms[0]), add(up, terms[1])
    down, up, sent[1] = join(down, up, sent[1])

    here = after(place, down)
    down, up = shift(down, -1), shift(up, 1)
    got.append(swap(sent[1], "yh"))
    (kept,) = make(here, 1, (1, Z), [lambda i, s: (s[0], 0)], [ORDER])
    down, up, near, kept, got[1] = join(down, up, near, kept, got[1])
    down = add(down, terms[2])
    down, sent[2], near = join(down, sent[2], near)

    near = near.reshape(2 * Z, -1, near.shape[-1])
    down = shift(down, -1)
    got.append(swap(sent[2], "yh"))
    context = attend(place, queries, doc_ids, near, swap(near, "c"))
    down, context, got[2] = join(down, context, got[2])
    first = add(down, up, terms[3])

    def second_term(order):
        return kept[order], got[order // 2][order % 2]

    going = chunk_of(first, 1 - high)
    down, up = add(*second_term(0)), add(*second_term(1))
    down, up, going, sent[3] = join(down, up, going, sent[3])
    down, up = shift(down, -1), shift(up, 1)
    got.append(swap(sent[3], "yh"))
    residual = lax.all_to_all(context, EXP, split_axis=0, concat_axis=1, tiled=True)
    down, up = join(down, up)
    down, up = add(down, *second_term(2)), add(up, *second_term(3))
    down, up, going = join(down, up, going)
    down, up, moved = shift(down, -1), shift(up, 1), swap(after(going, got[3]), "yh")
    down, up, got[3] = join(down, up, got[3])
    down, up = add(down, *second_term(4)), add(up, *second_term(5))
    down, up = join(down, up)
    down, up = shift(down, -1), shift(up, 1)
    down, up, moved = join(down, up, moved)
    down = add(down, *second_term(6))
    first = add(chunk_of(first, high), moved)
    down, residual = join(shift(down, -1), residual)
    second = add(down, up, *second_term(7))

    tokens = routes.shape[0]
    capacity = first.shape[0] // (2 * EXPERTS)
    mix = mixing(routes, route_weights, capacity)
    rows = jnp.concatenate([first, second], axis=1).reshape(2 * EXPERTS, capacity, -1)
    home = lax.all_to_all(rows, ("c",) + EXP, split_axis=0, concat_axis=0, tiled=True)
    home = home.reshape(2, EXPERTS * capacity, -1)
    both = jnp.einsum("tr,crn->tcn", mix, home, preferred_element_type=jnp.float32)
    mixed = (both[:tokens] + both[tokens:]).reshape(tokens, -1)
    moe_out = residual.astype(jnp.float32) + mixed
    return (context, moe_out.astype(jnp.bfloat16))


def chunk_of(array, at):
    return lax.dynamic_index_in_dim(array, at, 0, keepdims=False)


def mixing(routes, route_weights, capacity):
    flat = routes.reshape(-1)
    pairs = jnp.arange(flat.shape[0])
    same = (flat[:, None] == flat[None, :]) & (pairs[None, :] < pairs[:, None])
    slot = jnp.sum(same.astype(jnp.int32), axis=1).reshape(routes.shape)
    row = routes * capacity + slot
    hit = row[:, :, None] == jnp.arange(EXPERTS * capacity)[None, None, :]
    mix = jnp.sum(jnp.where(hit, route_weights[:, :, None], 0.0), axis=1)
    coarse = mix.astype(jnp.bfloat16)
    fine = (mix - coarse.astype(jnp.float32)).astype(jnp.bfloat16)
    return jnp.concatenate([coarse, fine], axis=0)


def solution(mesh):
    inner = Mesh(mesh.devices.reshape(SHAPE), AXES)
    in_specs = (
        P(CTX, EXP),
        P(CTX, EXP, None),
        P(CTX),
        P(EXP, None, CTX),
        P(EXP, CTX, None),
        P(CTX + EXP, None),
        P(CTX + EXP, None),
    )
    out_specs = (P(CTX, EXP), P(CTX + EXP, None))
    return jax.shard_map(shards, mesh=inner, in_specs=in_specs, out_specs=out_specs, check_vma=False)
```

```python
import math

import jax
import jax.numpy as jnp
from jax import lax
from jax.experimental import pallas as pl
from jax.experimental.pallas import tpu as pltpu
from jax.sharding import Mesh
from jax.sharding import PartitionSpec as P

AXES = ("yh", "z", "c", "x", "yl")
SHAPE = (2, 8, 2, 4, 2)
CTX = ("yh", "z", "c")
EXP = ("x", "yl")
Z = 8
EXPERTS = 8
PAD = 16
GROUPS = 2
ORDER = (4, 3, 5, 2, 6, 1, 7, 0)
PRODUCT_VMEM = 16 * 1024 * 1024
ATTENTION_VMEM = 24 * 1024 * 1024


def shift(value, step):
    return lax.ppermute(value, "z", [(i, (i + step) % Z) for i in range(Z)])


def swap(value, axis):
    return lax.ppermute(value, axis, [(0, 1), (1, 0)])


def after(value, *earlier):
    return lax.optimization_barrier((value,) + earlier)[0]


def attention_kernel(head, place, q_ref, doc_ref, a_ref, b_ref, o_ref, q_all, scores, top, total, acc):
    tokens = q_ref.shape[0]
    groups = q_ref.shape[1] // head
    high, along, core = place[0], place[1], place[2]
    mine = (high * Z + along) * 2 + core
    for g in range(groups):
        q_all[g * tokens : (g + 1) * tokens, :] = q_ref[:, g * head : (g + 1) * head]
    row = doc_ref[...].astype(jnp.float32)
    query_docs = jnp.transpose(jnp.broadcast_to(row, (tokens, tokens)))
    query_pos = lax.broadcasted_iota(jnp.int32, (tokens, tokens), 0) + mine * tokens
    lane = lax.broadcasted_iota(jnp.int32, (tokens, tokens), 1)
    top[...] = jnp.full_like(top, -1e30)
    total[...] = jnp.zeros_like(total)
    acc[...] = jnp.zeros_like(acc)
    arrays = ((a_ref, 0), (b_ref, 1))

    def origin(k, other_core):
        other_high = lax.rem(k, 2)
        high_at = high + other_high - 2 * high * other_high
        core_at = core + other_core - 2 * core * other_core
        return (high_at * Z + lax.div(k, 2)) * 2 + core_at

    for n, (ref, other_core) in enumerate(arrays):

        def score(k, carry, ref=ref, n=n, other_core=other_core):
            where = origin(k, other_core)

            @pl.when(where <= mine)
            def _():
                docs = ref[k, tokens : tokens + PAD, :tokens].astype(jnp.float32)[:1]
                allowed = (docs == query_docs) & (where * tokens + lane <= query_pos)
                s = lax.dot_general(
                    q_all[...],
                    ref[k, :tokens, :head],
                    (((1,), (1,)), ((), ())),
                    preferred_element_type=jnp.float32,
                )
                s = s.reshape(groups, tokens, tokens)
                s = jnp.where(allowed[None], s, jnp.float32(-1e30)).reshape(groups * tokens, tokens)
                scores[n * 2 * Z + k] = s
                top[...] = jnp.maximum(top[...], s)

            return carry

        lax.fori_loop(0, 2 * Z, score, 0)
    top[...] = jnp.broadcast_to(jnp.max(top[...], axis=1, keepdims=True), top.shape)
    factor = math.log2(math.e) / math.sqrt(head)
    for n, (ref, other_core) in enumerate(arrays):

        def mix(k, carry, ref=ref, n=n, other_core=other_core):
            where = origin(k, other_core)

            @pl.when(where <= mine)
            def _():
                weights = jnp.exp2((scores[n * 2 * Z + k] - top[...]) * factor)
                total[...] += weights
                acc[...] += jnp.dot(
                    weights.astype(jnp.bfloat16),
                    ref[k, :tokens, head:],
                    preferred_element_type=jnp.float32,
                )

            return carry

        lax.fori_loop(0, 2 * Z, mix, 0)
    out = acc[...] / jnp.sum(total[...], axis=1, keepdims=True)
    out = out.astype(o_ref.dtype)
    for g in range(groups):
        o_ref[:, g * head : (g + 1) * head] = out[g * tokens : (g + 1) * tokens, :]


def key_block(keys_values, doc_ids):
    tokens, width = doc_ids.shape[0], keys_values.shape[2]
    docs = jnp.pad(doc_ids.astype(jnp.bfloat16)[None, :], ((0, PAD - 1), (0, width - tokens)))
    return jnp.concatenate([keys_values, docs[:, None, :]], axis=0)


def attend(place, queries, doc_ids, near, far):
    tokens, width = doc_ids.shape[0], near.shape[-1]
    head = width // 2
    rows = queries.shape[1] // head * tokens
    spec = pl.BlockSpec(memory_space=pltpu.VMEM)
    return pl.pallas_call(
        lambda *refs: attention_kernel(head, *refs),
        out_shape=jax.ShapeDtypeStruct(queries.shape, jnp.bfloat16),
        in_specs=[pl.BlockSpec(memory_space=pltpu.SMEM)] + [spec] * 4,
        out_specs=spec,
        scratch_shapes=[
            pltpu.VMEM((rows, head), jnp.bfloat16),
            pltpu.VMEM((4 * Z, rows, tokens), jnp.float32),
            pltpu.VMEM((rows, tokens), jnp.float32),
            pltpu.VMEM((rows, tokens), jnp.float32),
            pltpu.VMEM((rows, head), jnp.float32),
        ],
        compiler_params=pltpu.CompilerParams(vmem_limit_bytes=ATTENTION_VMEM),
        name="attention",
    )(place, queries, doc_ids[None, :], near, far)


def slice_kernel(place, w_ref, o_ref):
    o_ref[...] = w_ref[...]


def other_columns(place, weight, columns, group):
    depth, strips = weight.shape[0], 4
    rows = depth // strips
    return pl.pallas_call(
        slice_kernel,
        out_shape=jax.ShapeDtypeStruct((depth, columns), weight.dtype),
        grid_spec=pltpu.PrefetchScalarGridSpec(
            num_scalar_prefetch=1,
            grid=(strips,),
            in_specs=[pl.BlockSpec((rows, columns), lambda i, s: (i, (1 - s[2]) * GROUPS + group))],
            out_specs=pl.BlockSpec((rows, columns), lambda i, s: (i, 0)),
        ),
        compiler_params=pltpu.CompilerParams(vmem_limit_bytes=PRODUCT_VMEM),
        name="columns",
    )(place, pltpu.with_memory_space_constraint(weight, pltpu.HBM))


def product_kernel(count, offsets, place, *refs):
    depth = refs[0].shape[-1]
    wa_ref, wb_ref = refs[2 * count : 2 * count + 2]
    a = jnp.concatenate([ref[...].reshape(-1, depth) for ref in refs[:count]], axis=0)
    b = jnp.concatenate([ref[...].reshape(-1, depth) for ref in refs[count : 2 * count]], axis=0)
    out = jnp.dot(a, wa_ref[...], preferred_element_type=jnp.float32)
    out += jnp.dot(b, wb_ref[...], preferred_element_type=jnp.float32)
    out = out.astype(jnp.bfloat16)
    if offsets is None:
        o_refs = refs[2 * count + 2 :]
        rows = out.shape[0] // len(o_refs)
        for i, o_ref in enumerate(o_refs):
            o_ref[...] = out[i * rows : (i + 1) * rows].reshape(o_ref.shape)
    else:
        o_refs, chunks = refs[2 * count + 2 : -1], refs[-1]
        chunks[...] = out.reshape(chunks.shape)
        for o_ref, picks in zip(o_refs, offsets):
            for k, offset in enumerate(picks):
                o_ref[k] = chunks[lax.rem(place[1] + offset, Z)].reshape(o_ref.shape[1:])


def product(place, acts, acts_other, weight, other, first, block, picks, steps, offsets, split):
    depth, rows = acts.shape[-1], acts.shape[2]
    columns = other.shape[1]
    tile = columns // 2
    half, start = weight.shape[1] // (2 * tile), first * 2
    specs = [pl.BlockSpec(block + (rows, depth), lambda j, i, s, pick=pick: pick(i, s) + (0, 0)) for pick in picks]
    if offsets is None:
        shapes, blocks = [block + (rows, columns)] * len(picks), [block + (rows, tile)] * len(picks)
        scratch = []
    else:
        split = (steps,) if split else ()
        shapes = [(len(o),) + split + (rows, columns) for o in offsets]
        blocks = [(len(o),) + (1,) * len(split) + (rows, tile) for o in offsets]
        scratch = [pltpu.VMEM(block[1:] + (rows, tile), jnp.bfloat16)]

    def out_map(rank):
        if rank == 3:
            return lambda j, i, s: (0, 0, j)
        return lambda j, i, s: (0, i, 0, j)

    weight = pltpu.with_memory_space_constraint(weight, pltpu.HBM)
    return pl.pallas_call(
        lambda *refs: product_kernel(len(picks), offsets, *refs),
        out_shape=[jax.ShapeDtypeStruct(shape, jnp.bfloat16) for shape in shapes],
        grid_spec=pltpu.PrefetchScalarGridSpec(
            num_scalar_prefetch=1,
            grid=(2, steps),
            in_specs=specs
            + specs
            + [
                pl.BlockSpec((depth, tile), lambda j, i, s: (0, s[2] * half + start + j)),
                pl.BlockSpec((depth, tile), lambda j, i, s: (0, j)),
            ],
            out_specs=[pl.BlockSpec(b, out_map(len(b))) for b in blocks],
            scratch_shapes=scratch,
        ),
        compiler_params=pltpu.CompilerParams(vmem_limit_bytes=PRODUCT_VMEM),
        name="product",
    )(place, *([acts] * len(picks)), *([acts_other] * len(picks)), weight, other)


def add(*terms):
    total = terms[0].astype(jnp.float32)
    for term in terms[1:]:
        total = total + term.astype(jnp.float32)
    return total.astype(jnp.bfloat16)


def join(*values):
    return lax.optimization_barrier(values)


def shards(queries, keys_values, doc_ids, gate_up, down_weight, routes, route_weights):
    high, along, core = (lax.axis_index(name).astype(jnp.int32) for name in CTX)
    place = jnp.stack([high, along, core])
    weight = down_weight[0]
    columns = weight.shape[1] // (2 * GROUPS)
    depth = weight.shape[0]
    acts = gate_up[0].reshape(2, Z, -1, depth)

    acts_other = swap(gate_up[0], "c")
    part = other_columns(place, weight, columns, 0)
    other = [swap(part, "c")]
    acts_other = acts_other.reshape(2, Z, -1, depth)

    def make(where, group, block, picks, offsets=None):
        return product(where, acts, acts_other, weight, other[group], group, block, picks, 1, offsets, False)

    def first_terms(where, orders):
        picks = [lambda i, s, k=ORDER[order]: (0, lax.rem(s[1] + k, Z)) for order in orders]
        return [term[:, 0] for term in make(where, 0, (2, 1), picks)]

    down, up = first_terms(place, (0, 1))
    other.append(swap(other_columns(after(place, down), weight, columns, 1), "c"))
    block = key_block(keys_values, after(doc_ids, down))
    pair = jnp.concatenate([block, swap(block, "yh")], axis=0)
    near = lax.all_gather(pair, "z", axis=0, tiled=True)
    here = after(place, block)
    down, up = shift(down, -1), shift(up, 1)
    down_term, up_term = first_terms(here, (2, 3))
    down, up, down_term, up_term, pair = join(down, up, down_term, up_term, pair)
    down, up = add(down, down_term), add(up, up_term)
    down, up = join(down, up)

    here = after(place, down)
    down, up = shift(down, -1), shift(up, 1)
    sent = list(make(here, 1, (1, Z), [lambda i, s: (1 - s[0], 0)], [ORDER[:4], ORDER[4:6], ORDER[6:]]))
    got = [swap(sent[0], "yh")]
    terms = first_terms(after(place, sent[0]), (4, 5, 6, 7))
    down, up, *terms = join(down, up, *terms)
    down, up = add(down, terms[0]), add(up, terms[1])
    down, up = join(down, up)

    here = after(place, down)
    down, up = shift(down, -1), shift(up, 1)
    (kept,) = make(here, 1, (1, Z), [lambda i, s: (s[0], 0)], [ORDER])
    down, up, near, kept, got[0] = join(down, up, near, kept, got[0])
    down = add(down, terms[2])
    down, sent[1], near = join(down, sent[1], near)

    near = near.reshape(2 * Z, -1, near.shape[-1])
    down = shift(down, -1)
    got.append(swap(sent[1], "yh"))
    context = attend(place, queries, doc_ids, near, swap(near, "c"))
    down, context = join(down, context)
    first = add(down, up, terms[3])

    def second_term(order):
        piece = 0 if order < 4 else order // 2 - 1
        return kept[order], got[piece][order if order < 4 else order % 2]

    going = chunk_of(first, 1 - high)
    down, up = add(*second_term(0)), add(*second_term(1))
    down, up, going = join(down, up, going)
    down, up, moved = shift(down, -1), shift(up, 1), swap(going, "yh")
    residual = lax.all_to_all(context, EXP, split_axis=0, concat_axis=1, tiled=True)
    down, up, got[1] = join(down, up, got[1])
    down, up = add(down, *second_term(2)), add(up, *second_term(3))
    down, up, sent[2] = join(down, up, sent[2])
    down, up = shift(down, -1), shift(up, 1)
    got.append(swap(sent[2], "yh"))
    down, up, moved = join(down, up, moved)
    down, up = add(down, *second_term(4)), add(up, *second_term(5))
    down, up = join(down, up)
    down, up = shift(down, -1), shift(up, 1)
    down, up, got[2] = join(down, up, got[2])
    down = add(down, *second_term(6))
    first = add(chunk_of(first, high), after(moved, residual))
    down, residual = join(shift(down, -1), residual)
    second = add(down, up, *second_term(7))

    tokens = routes.shape[0]
    capacity = first.shape[0] // (2 * EXPERTS)
    mix = mixing(routes, route_weights, capacity)
    rows = jnp.concatenate([first, second], axis=1).reshape(2 * EXPERTS, capacity, -1)
    home = lax.all_to_all(rows, ("c",) + EXP, split_axis=0, concat_axis=0, tiled=True)
    home = home.reshape(2, EXPERTS * capacity, -1)
    both = jnp.einsum("tr,crn->tcn", mix, home, preferred_element_type=jnp.float32)
    mixed = (both[:tokens] + both[tokens:]).reshape(tokens, -1)
    moe_out = residual.astype(jnp.float32) + mixed
    return (context, moe_out.astype(jnp.bfloat16))


def chunk_of(array, at):
    return lax.dynamic_index_in_dim(array, at, 0, keepdims=False)


def mixing(routes, route_weights, capacity):
    flat = routes.reshape(-1)
    pairs = jnp.arange(flat.shape[0])
    same = (flat[:, None] == flat[None, :]) & (pairs[None, :] < pairs[:, None])
    slot = jnp.sum(same.astype(jnp.int32), axis=1).reshape(routes.shape)
    row = routes * capacity + slot
    hit = row[:, :, None] == jnp.arange(EXPERTS * capacity)[None, None, :]
    mix = jnp.sum(jnp.where(hit, route_weights[:, :, None], 0.0), axis=1)
    coarse = mix.astype(jnp.bfloat16)
    fine = (mix - coarse.astype(jnp.float32)).astype(jnp.bfloat16)
    return jnp.concatenate([coarse, fine], axis=0)


def solution(mesh):
    inner = Mesh(mesh.devices.reshape(SHAPE), AXES)
    in_specs = (
        P(CTX, EXP),
        P(CTX, EXP, None),
        P(CTX),
        P(EXP, None, CTX),
        P(EXP, CTX, None),
        P(CTX + EXP, None),
        P(CTX + EXP, None),
    )
    out_specs = (P(CTX, EXP), P(CTX + EXP, None))
    return jax.shard_map(shards, mesh=inner, in_specs=in_specs, out_specs=out_specs, check_vma=False)
```

```python
import math

import jax
import jax.numpy as jnp
from jax import lax
from jax.experimental import pallas as pl
from jax.experimental.pallas import tpu as pltpu
from jax.sharding import Mesh
from jax.sharding import PartitionSpec as P

AXES = ("yh", "z", "c", "x", "yl")
SHAPE = (2, 8, 2, 4, 2)
CTX = ("yh", "z", "c")
EXP = ("x", "yl")
Z = 8
EXPERTS = 8
PAD = 16
GROUPS = 2
ORDER = (4, 3, 5, 2, 6, 1, 7, 0)
PRODUCT_VMEM = 16 * 1024 * 1024
ATTENTION_VMEM = 24 * 1024 * 1024


def shift(value, step):
    return lax.ppermute(value, "z", [(i, (i + step) % Z) for i in range(Z)])


def swap(value, axis):
    return lax.ppermute(value, axis, [(0, 1), (1, 0)])


def after(value, *earlier):
    return lax.optimization_barrier((value,) + earlier)[0]


def attention_kernel(head, place, q_ref, doc_ref, a_ref, b_ref, o_ref, q_all, scores, top, total, acc):
    tokens = q_ref.shape[0]
    groups = q_ref.shape[1] // head
    high, along, core = place[0], place[1], place[2]
    mine = (high * Z + along) * 2 + core
    for g in range(groups):
        q_all[g * tokens : (g + 1) * tokens, :] = q_ref[:, g * head : (g + 1) * head]
    row = doc_ref[...].astype(jnp.float32)
    query_docs = jnp.transpose(jnp.broadcast_to(row, (tokens, tokens)))
    query_pos = lax.broadcasted_iota(jnp.int32, (tokens, tokens), 0) + mine * tokens
    lane = lax.broadcasted_iota(jnp.int32, (tokens, tokens), 1)
    top[...] = jnp.full_like(top, -1e30)
    total[...] = jnp.zeros_like(total)
    acc[...] = jnp.zeros_like(acc)
    arrays = ((a_ref, 0), (b_ref, 1))

    def origin(k, other_core):
        other_high = lax.rem(k, 2)
        high_at = high + other_high - 2 * high * other_high
        core_at = core + other_core - 2 * core * other_core
        return (high_at * Z + lax.div(k, 2)) * 2 + core_at

    for n, (ref, other_core) in enumerate(arrays):

        def score(k, carry, ref=ref, n=n, other_core=other_core):
            where = origin(k, other_core)

            @pl.when(where <= mine)
            def _():
                docs = ref[k, tokens : tokens + PAD, :tokens].astype(jnp.float32)[:1]
                allowed = (docs == query_docs) & (where * tokens + lane <= query_pos)
                s = lax.dot_general(
                    q_all[...],
                    ref[k, :tokens, :head],
                    (((1,), (1,)), ((), ())),
                    preferred_element_type=jnp.float32,
                )
                s = s.reshape(groups, tokens, tokens)
                s = jnp.where(allowed[None], s, jnp.float32(-1e30)).reshape(groups * tokens, tokens)
                scores[n * 2 * Z + k] = s
                top[...] = jnp.maximum(top[...], s)

            return carry

        lax.fori_loop(0, 2 * Z, score, 0)
    top[...] = jnp.broadcast_to(jnp.max(top[...], axis=1, keepdims=True), top.shape)
    factor = math.log2(math.e) / math.sqrt(head)
    for n, (ref, other_core) in enumerate(arrays):

        def mix(k, carry, ref=ref, n=n, other_core=other_core):
            where = origin(k, other_core)

            @pl.when(where <= mine)
            def _():
                weights = jnp.exp2((scores[n * 2 * Z + k] - top[...]) * factor)
                total[...] += weights
                acc[...] += jnp.dot(
                    weights.astype(jnp.bfloat16),
                    ref[k, :tokens, head:],
                    preferred_element_type=jnp.float32,
                )

            return carry

        lax.fori_loop(0, 2 * Z, mix, 0)
    out = acc[...] / jnp.sum(total[...], axis=1, keepdims=True)
    out = out.astype(o_ref.dtype)
    for g in range(groups):
        o_ref[:, g * head : (g + 1) * head] = out[g * tokens : (g + 1) * tokens, :]


def key_block(keys_values, doc_ids):
    tokens, width = doc_ids.shape[0], keys_values.shape[2]
    docs = jnp.pad(doc_ids.astype(jnp.bfloat16)[None, :], ((0, PAD - 1), (0, width - tokens)))
    return jnp.concatenate([keys_values, docs[:, None, :]], axis=0)


def attend(place, queries, doc_ids, near, far):
    tokens, width = doc_ids.shape[0], near.shape[-1]
    head = width // 2
    rows = queries.shape[1] // head * tokens
    spec = pl.BlockSpec(memory_space=pltpu.VMEM)
    return pl.pallas_call(
        lambda *refs: attention_kernel(head, *refs),
        out_shape=jax.ShapeDtypeStruct(queries.shape, jnp.bfloat16),
        in_specs=[pl.BlockSpec(memory_space=pltpu.SMEM)] + [spec] * 4,
        out_specs=spec,
        scratch_shapes=[
            pltpu.VMEM((rows, head), jnp.bfloat16),
            pltpu.VMEM((4 * Z, rows, tokens), jnp.float32),
            pltpu.VMEM((rows, tokens), jnp.float32),
            pltpu.VMEM((rows, tokens), jnp.float32),
            pltpu.VMEM((rows, head), jnp.float32),
        ],
        compiler_params=pltpu.CompilerParams(vmem_limit_bytes=ATTENTION_VMEM),
        name="attention",
    )(place, queries, doc_ids[None, :], near, far)


def slice_kernel(place, w_ref, o_ref):
    o_ref[...] = w_ref[...]


def other_columns(place, weight, columns, group):
    depth, strips = weight.shape[0], 4
    rows = depth // strips
    return pl.pallas_call(
        slice_kernel,
        out_shape=jax.ShapeDtypeStruct((depth, columns), weight.dtype),
        grid_spec=pltpu.PrefetchScalarGridSpec(
            num_scalar_prefetch=1,
            grid=(strips,),
            in_specs=[pl.BlockSpec((rows, columns), lambda i, s: (i, (1 - s[2]) * GROUPS + group))],
            out_specs=pl.BlockSpec((rows, columns), lambda i, s: (i, 0)),
        ),
        compiler_params=pltpu.CompilerParams(vmem_limit_bytes=PRODUCT_VMEM),
        name="columns",
    )(place, pltpu.with_memory_space_constraint(weight, pltpu.HBM))


def product_kernel(count, offsets, place, *refs):
    depth = refs[0].shape[-1]
    wa_ref, wb_ref = refs[2 * count : 2 * count + 2]
    a = jnp.concatenate([ref[...].reshape(-1, depth) for ref in refs[:count]], axis=0)
    b = jnp.concatenate([ref[...].reshape(-1, depth) for ref in refs[count : 2 * count]], axis=0)
    out = jnp.dot(a, wa_ref[...], preferred_element_type=jnp.float32)
    out += jnp.dot(b, wb_ref[...], preferred_element_type=jnp.float32)
    out = out.astype(jnp.bfloat16)
    if offsets is None:
        o_refs = refs[2 * count + 2 :]
        rows = out.shape[0] // len(o_refs)
        for i, o_ref in enumerate(o_refs):
            o_ref[...] = out[i * rows : (i + 1) * rows].reshape(o_ref.shape)
    else:
        o_refs, chunks = refs[2 * count + 2 : -1], refs[-1]
        chunks[...] = out.reshape(chunks.shape)
        for o_ref, picks in zip(o_refs, offsets):
            for k, offset in enumerate(picks):
                o_ref[k] = chunks[lax.rem(place[1] + offset, Z)].reshape(o_ref.shape[1:])


def product(place, acts, acts_other, weight, other, first, block, picks, steps, offsets, split):
    depth, rows = acts.shape[-1], acts.shape[2]
    columns = other.shape[1]
    tile = columns // 2
    half, start = weight.shape[1] // (2 * tile), first * 2
    specs = [pl.BlockSpec(block + (rows, depth), lambda j, i, s, pick=pick: pick(i, s) + (0, 0)) for pick in picks]
    if offsets is None:
        shapes, blocks = [block + (rows, columns)] * len(picks), [block + (rows, tile)] * len(picks)
        scratch = []
    else:
        split = (steps,) if split else ()
        shapes = [(len(o),) + split + (rows, columns) for o in offsets]
        blocks = [(len(o),) + (1,) * len(split) + (rows, tile) for o in offsets]
        scratch = [pltpu.VMEM(block[1:] + (rows, tile), jnp.bfloat16)]

    def out_map(rank):
        if rank == 3:
            return lambda j, i, s: (0, 0, j)
        return lambda j, i, s: (0, i, 0, j)

    weight = pltpu.with_memory_space_constraint(weight, pltpu.HBM)
    return pl.pallas_call(
        lambda *refs: product_kernel(len(picks), offsets, *refs),
        out_shape=[jax.ShapeDtypeStruct(shape, jnp.bfloat16) for shape in shapes],
        grid_spec=pltpu.PrefetchScalarGridSpec(
            num_scalar_prefetch=1,
            grid=(2, steps),
            in_specs=specs
            + specs
            + [
                pl.BlockSpec((depth, tile), lambda j, i, s: (0, s[2] * half + start + j)),
                pl.BlockSpec((depth, tile), lambda j, i, s: (0, j)),
            ],
            out_specs=[pl.BlockSpec(b, out_map(len(b))) for b in blocks],
            scratch_shapes=scratch,
        ),
        compiler_params=pltpu.CompilerParams(vmem_limit_bytes=PRODUCT_VMEM),
        name="product",
    )(place, *([acts] * len(picks)), *([acts_other] * len(picks)), weight, other)


def add(*terms):
    total = terms[0].astype(jnp.float32)
    for term in terms[1:]:
        total = total + term.astype(jnp.float32)
    return total.astype(jnp.bfloat16)


def join(*values):
    return lax.optimization_barrier(values)


def shards(queries, keys_values, doc_ids, gate_up, down_weight, routes, route_weights):
    high, along, core = (lax.axis_index(name).astype(jnp.int32) for name in CTX)
    place = jnp.stack([high, along, core])
    weight = down_weight[0]
    columns = weight.shape[1] // (2 * GROUPS)
    depth = weight.shape[0]
    acts = gate_up[0].reshape(2, Z, -1, depth)

    acts_other = swap(gate_up[0], "c")
    part = other_columns(place, weight, columns, 0)
    other = [swap(part, "c")]
    acts_other = acts_other.reshape(2, Z, -1, depth)

    def make(where, group, block, picks, offsets=None):
        return product(where, acts, acts_other, weight, other[group], group, block, picks, 1, offsets, False)

    def first_terms(where, orders):
        picks = [lambda i, s, k=ORDER[order]: (0, lax.rem(s[1] + k, Z)) for order in orders]
        return [term[:, 0] for term in make(where, 0, (2, 1), picks)]

    down, up = first_terms(place, (0, 1))
    other.append(swap(other_columns(after(place, down), weight, columns, 1), "c"))
    block = key_block(keys_values, after(doc_ids, down))
    pair = jnp.concatenate([block, swap(block, "yh")], axis=0)
    near = lax.all_gather(pair, "z", axis=0, tiled=True)
    here = after(place, block)
    down, up = shift(down, -1), shift(up, 1)
    down_term, up_term = first_terms(here, (2, 3))
    down, up, down_term, up_term, pair = join(down, up, down_term, up_term, pair)
    down, up = add(down, down_term), add(up, up_term)
    down, up = join(down, up)

    here = after(place, down)
    down, up = shift(down, -1), shift(up, 1)
    sent = list(make(here, 1, (1, Z), [lambda i, s: (1 - s[0], 0)], [ORDER[:4], ORDER[4:6], ORDER[6:]]))
    got = [swap(sent[0], "yh")]
    terms = first_terms(after(place, sent[0]), (4, 5, 6, 7))
    down, up, *terms = join(down, up, *terms)
    down, up = add(down, terms[0]), add(up, terms[1])
    down, up = join(down, up)

    here = after(place, down)
    down, up = shift(down, -1), shift(up, 1)
    (kept,) = make(here, 1, (1, Z), [lambda i, s: (s[0], 0)], [ORDER])
    down, up, near, kept, got[0] = join(down, up, near, kept, got[0])
    down = add(down, terms[2])
    down, sent[1], near = join(down, sent[1], near)

    near = near.reshape(2 * Z, -1, near.shape[-1])
    down = shift(down, -1)
    got.append(swap(sent[1], "yh"))
    context = attend(place, queries, doc_ids, near, swap(near, "c"))
    down, context = join(down, context)
    first = add(down, up, terms[3])

    def second_term(order):
        piece = 0 if order < 4 else order // 2 - 1
        return kept[order], got[piece][order if order < 4 else order % 2]

    going = chunk_of(first, 1 - high)
    down, up = add(*second_term(0)), add(*second_term(1))
    down, up, going = join(down, up, going)
    down, up = shift(down, -1), shift(up, 1)
    last = jnp.concatenate([sent[2], going[None]], axis=0)
    residual = lax.all_to_all(context, EXP, split_axis=0, concat_axis=1, tiled=True)
    down, up, got[1] = join(down, up, got[1])
    down, up = add(down, *second_term(2)), add(up, *second_term(3))
    down, up, last = join(down, up, last)
    down, up = shift(down, -1), shift(up, 1)
    last = swap(last, "yh")
    down, up = join(down, up)
    down, up = add(down, *second_term(4)), add(up, *second_term(5))
    down, up = join(down, up)
    down, up = shift(down, -1), shift(up, 1)
    down, up, last = join(down, up, last)
    got.append(last[:2])
    moved = last[2]
    down = add(down, *second_term(6))
    first = add(chunk_of(first, high), after(moved, residual))
    down, residual = join(shift(down, -1), residual)
    second = add(down, up, *second_term(7))

    tokens = routes.shape[0]
    capacity = first.shape[0] // (2 * EXPERTS)
    mix = mixing(routes, route_weights, capacity)
    rows = jnp.concatenate([first, second], axis=1).reshape(2 * EXPERTS, capacity, -1)
    home = lax.all_to_all(rows, ("c",) + EXP, split_axis=0, concat_axis=0, tiled=True)
    home = home.reshape(2, EXPERTS * capacity, -1)
    both = jnp.einsum("tr,crn->tcn", mix, home, preferred_element_type=jnp.float32)
    mixed = (both[:tokens] + both[tokens:]).reshape(tokens, -1)
    moe_out = residual.astype(jnp.float32) + mixed
    return (context, moe_out.astype(jnp.bfloat16))


def chunk_of(array, at):
    return lax.dynamic_index_in_dim(array, at, 0, keepdims=False)


def mixing(routes, route_weights, capacity):
    flat = routes.reshape(-1)
    pairs = jnp.arange(flat.shape[0])
    same = (flat[:, None] == flat[None, :]) & (pairs[None, :] < pairs[:, None])
    slot = jnp.sum(same.astype(jnp.int32), axis=1).reshape(routes.shape)
    row = routes * capacity + slot
    hit = row[:, :, None] == jnp.arange(EXPERTS * capacity)[None, None, :]
    mix = jnp.sum(jnp.where(hit, route_weights[:, :, None], 0.0), axis=1)
    coarse = mix.astype(jnp.bfloat16)
    fine = (mix - coarse.astype(jnp.float32)).astype(jnp.bfloat16)
    return jnp.concatenate([coarse, fine], axis=0)


def solution(mesh):
    inner = Mesh(mesh.devices.reshape(SHAPE), AXES)
    in_specs = (
        P(CTX, EXP),
        P(CTX, EXP, None),
        P(CTX),
        P(EXP, None, CTX),
        P(EXP, CTX, None),
        P(CTX + EXP, None),
        P(CTX + EXP, None),
    )
    out_specs = (P(CTX, EXP), P(CTX + EXP, None))
    return jax.shard_map(shards, mesh=inner, in_specs=in_specs, out_specs=out_specs, check_vma=False)
```

```python
import math

import jax
import jax.numpy as jnp
from jax import lax
from jax.experimental import pallas as pl
from jax.experimental.pallas import tpu as pltpu
from jax.sharding import Mesh
from jax.sharding import PartitionSpec as P

AXES = ("yh", "z", "c", "x", "yl")
SHAPE = (2, 8, 2, 4, 2)
CTX = ("yh", "z", "c")
EXP = ("x", "yl")
Z = 8
EXPERTS = 8
PAD = 16
SPLIT = 8
GROUPS = 2
ORDER = (4, 3, 5, 2, 6, 1, 7, 0)
PRODUCT_VMEM = 16 * 1024 * 1024
ATTENTION_VMEM = 24 * 1024 * 1024


def shift(value, step):
    return lax.ppermute(value, "z", [(i, (i + step) % Z) for i in range(Z)])


def swap(value, axis):
    return lax.ppermute(value, axis, [(0, 1), (1, 0)])


def after(value, *earlier):
    return lax.optimization_barrier((value,) + earlier)[0]


def attention_kernel(head, place, q_ref, doc_ref, a_ref, b_ref, o_ref, q_all, scores, top, total, acc):
    tokens = q_ref.shape[0]
    groups = q_ref.shape[1] // head
    high, along, core = place[0], place[1], place[2]
    mine = (high * Z + along) * 2 + core
    for g in range(groups):
        q_all[g * tokens : (g + 1) * tokens, :] = q_ref[:, g * head : (g + 1) * head]
    row = doc_ref[...].astype(jnp.float32)
    query_docs = jnp.transpose(jnp.broadcast_to(row, (tokens, tokens)))
    query_pos = lax.broadcasted_iota(jnp.int32, (tokens, tokens), 0) + mine * tokens
    lane = lax.broadcasted_iota(jnp.int32, (tokens, tokens), 1)
    top[...] = jnp.full_like(top, -1e30)
    total[...] = jnp.zeros_like(total)
    acc[...] = jnp.zeros_like(acc)
    arrays = ((a_ref, 0), (b_ref, 1))

    def origin(k, other_core):
        other_high = lax.rem(k, 2)
        high_at = high + other_high - 2 * high * other_high
        core_at = core + other_core - 2 * core * other_core
        return (high_at * Z + lax.div(k, 2)) * 2 + core_at

    for n, (ref, other_core) in enumerate(arrays):

        def score(k, carry, ref=ref, n=n, other_core=other_core):
            where = origin(k, other_core)

            @pl.when(where <= mine)
            def _():
                docs = ref[k, tokens : tokens + PAD, :tokens].astype(jnp.float32)[:1]
                allowed = (docs == query_docs) & (where * tokens + lane <= query_pos)
                s = lax.dot_general(
                    q_all[...],
                    ref[k, :tokens, :head],
                    (((1,), (1,)), ((), ())),
                    preferred_element_type=jnp.float32,
                )
                s = s.reshape(groups, tokens, tokens)
                s = jnp.where(allowed[None], s, jnp.float32(-1e30)).reshape(groups * tokens, tokens)
                scores[n * 2 * Z + k] = s
                top[...] = jnp.maximum(top[...], s)

            return carry

        lax.fori_loop(0, 2 * Z, score, 0)
    top[...] = jnp.broadcast_to(jnp.max(top[...], axis=1, keepdims=True), top.shape)
    factor = math.log2(math.e) / math.sqrt(head)
    for n, (ref, other_core) in enumerate(arrays):

        def mix(k, carry, ref=ref, n=n, other_core=other_core):
            where = origin(k, other_core)

            @pl.when(where <= mine)
            def _():
                weights = jnp.exp2((scores[n * 2 * Z + k] - top[...]) * factor)
                total[...] += weights
                acc[...] += jnp.dot(
                    weights.astype(jnp.bfloat16),
                    ref[k, :tokens, head:],
                    preferred_element_type=jnp.float32,
                )

            return carry

        lax.fori_loop(0, 2 * Z, mix, 0)
    out = acc[...] / jnp.sum(total[...], axis=1, keepdims=True)
    out = out.astype(o_ref.dtype)
    for g in range(groups):
        o_ref[:, g * head : (g + 1) * head] = out[g * tokens : (g + 1) * tokens, :]


def key_block(keys_values, doc_ids):
    tokens, width = doc_ids.shape[0], keys_values.shape[2]
    docs = jnp.pad(doc_ids.astype(jnp.bfloat16)[None, :], ((0, PAD - 1), (0, width - tokens)))
    return jnp.concatenate([keys_values, docs[:, None, :]], axis=0)


def attend(place, queries, doc_ids, near, far):
    tokens, width = doc_ids.shape[0], near.shape[-1]
    head = width // 2
    rows = queries.shape[1] // head * tokens
    spec = pl.BlockSpec(memory_space=pltpu.VMEM)
    return pl.pallas_call(
        lambda *refs: attention_kernel(head, *refs),
        out_shape=jax.ShapeDtypeStruct(queries.shape, jnp.bfloat16),
        in_specs=[pl.BlockSpec(memory_space=pltpu.SMEM)] + [spec] * 4,
        out_specs=spec,
        scratch_shapes=[
            pltpu.VMEM((rows, head), jnp.bfloat16),
            pltpu.VMEM((4 * Z, rows, tokens), jnp.float32),
            pltpu.VMEM((rows, tokens), jnp.float32),
            pltpu.VMEM((rows, tokens), jnp.float32),
            pltpu.VMEM((rows, head), jnp.float32),
        ],
        compiler_params=pltpu.CompilerParams(vmem_limit_bytes=ATTENTION_VMEM),
        name="attention",
    )(place, queries, doc_ids[None, :], near, far)


def slice_kernel(place, w_ref, o_ref):
    o_ref[...] = w_ref[...]


def other_columns(place, weight, columns, group):
    depth, strips = weight.shape[0], 4
    rows = depth // strips
    return pl.pallas_call(
        slice_kernel,
        out_shape=jax.ShapeDtypeStruct((depth, columns), weight.dtype),
        grid_spec=pltpu.PrefetchScalarGridSpec(
            num_scalar_prefetch=1,
            grid=(strips,),
            in_specs=[pl.BlockSpec((rows, columns), lambda i, s: (i, (1 - s[2]) * GROUPS + group))],
            out_specs=pl.BlockSpec((rows, columns), lambda i, s: (i, 0)),
        ),
        compiler_params=pltpu.CompilerParams(vmem_limit_bytes=PRODUCT_VMEM),
        name="columns",
    )(place, pltpu.with_memory_space_constraint(weight, pltpu.HBM))


def product_kernel(count, offsets, place, *refs):
    depth = refs[0].shape[-1]
    wa_ref, wb_ref = refs[2 * count : 2 * count + 2]
    a = jnp.concatenate([ref[...].reshape(-1, depth) for ref in refs[:count]], axis=0)
    b = jnp.concatenate([ref[...].reshape(-1, depth) for ref in refs[count : 2 * count]], axis=0)
    out = jnp.dot(a, wa_ref[...], preferred_element_type=jnp.float32)
    out += jnp.dot(b, wb_ref[...], preferred_element_type=jnp.float32)
    out = out.astype(jnp.bfloat16)
    if offsets is None:
        o_refs = refs[2 * count + 2 :]
        rows = out.shape[0] // len(o_refs)
        for i, o_ref in enumerate(o_refs):
            o_ref[...] = out[i * rows : (i + 1) * rows].reshape(o_ref.shape)
    else:
        o_refs, chunks = refs[2 * count + 2 : -1], refs[-1]
        chunks[...] = out.reshape(chunks.shape)
        for o_ref, picks in zip(o_refs, offsets):
            for k, offset in enumerate(picks):
                o_ref[k] = chunks[lax.rem(place[1] + offset, Z)].reshape(o_ref.shape[1:])


def product(place, acts, acts_other, weight, other, first, block, picks, steps, offsets, split):
    depth, rows = acts.shape[-1], acts.shape[2]
    columns = other.shape[1]
    tile = columns // 2
    half, start = weight.shape[1] // (2 * tile), first * 2
    specs = [pl.BlockSpec(block + (rows, depth), lambda j, i, s, pick=pick: pick(i, s) + (0, 0)) for pick in picks]
    if offsets is None:
        shapes, blocks = [block + (rows, columns)] * len(picks), [block + (rows, tile)] * len(picks)
        scratch = []
    else:
        split = (steps,) if split else ()
        shapes = [(len(o),) + split + (rows, columns) for o in offsets]
        blocks = [(len(o),) + (1,) * len(split) + (rows, tile) for o in offsets]
        scratch = [pltpu.VMEM(block[1:] + (rows, tile), jnp.bfloat16)]

    def out_map(rank):
        if rank == 3:
            return lambda j, i, s: (0, 0, j)
        return lambda j, i, s: (0, i, 0, j)

    weight = pltpu.with_memory_space_constraint(weight, pltpu.HBM)
    return pl.pallas_call(
        lambda *refs: product_kernel(len(picks), offsets, *refs),
        out_shape=[jax.ShapeDtypeStruct(shape, jnp.bfloat16) for shape in shapes],
        grid_spec=pltpu.PrefetchScalarGridSpec(
            num_scalar_prefetch=1,
            grid=(2, steps),
            in_specs=specs
            + specs
            + [
                pl.BlockSpec((depth, tile), lambda j, i, s: (0, s[2] * half + start + j)),
                pl.BlockSpec((depth, tile), lambda j, i, s: (0, j)),
            ],
            out_specs=[pl.BlockSpec(b, out_map(len(b))) for b in blocks],
            scratch_shapes=scratch,
        ),
        compiler_params=pltpu.CompilerParams(vmem_limit_bytes=PRODUCT_VMEM),
        name="product",
    )(place, *([acts] * len(picks)), *([acts_other] * len(picks)), weight, other)


def add(*terms):
    total = terms[0].astype(jnp.float32)
    for term in terms[1:]:
        total = total + term.astype(jnp.float32)
    return total.astype(jnp.bfloat16)


def join(*values):
    return lax.optimization_barrier(values)


def shards(queries, keys_values, doc_ids, gate_up, down_weight, routes, route_weights):
    high, along, core = (lax.axis_index(name).astype(jnp.int32) for name in CTX)
    place = jnp.stack([high, along, core])
    weight = down_weight[0]
    columns = weight.shape[1] // (2 * GROUPS)
    depth = weight.shape[0]
    acts = gate_up[0].reshape(2, Z, -1, depth)

    acts_other = swap(gate_up[0], "c")
    part = other_columns(place, weight, columns, 0)
    other = [swap(part, "c")]
    acts_other = acts_other.reshape(2, Z, -1, depth)

    def make(where, group, block, picks, offsets=None):
        return product(where, acts, acts_other, weight, other[group], group, block, picks, 1, offsets, False)

    def first_terms(where, orders):
        picks = [lambda i, s, k=ORDER[order]: (0, lax.rem(s[1] + k, Z)) for order in orders]
        return [term[:, 0] for term in make(where, 0, (2, 1), picks)]

    down, up = first_terms(place, (0, 1))
    other.append(swap(other_columns(after(place, down), weight, columns, 1), "c"))
    block = key_block(keys_values, after(doc_ids, down))
    pair = jnp.concatenate([block, swap(block, "yh")], axis=0)
    near = lax.all_gather(pair, "z", axis=0, tiled=True)
    here = after(place, block)
    down, up = shift(down, -1), shift(up, 1)
    down_term, up_term = first_terms(here, (2, 3))
    down, up, down_term, up_term, pair = join(down, up, down_term, up_term, pair)
    down, up = add(down, down_term), add(up, up_term)
    down, up = join(down, up)

    here = after(place, down)
    down, up = shift(down, -1), shift(up, 1)
    sent = list(make(here, 1, (1, Z), [lambda i, s: (1 - s[0], 0)], [ORDER[:4], ORDER[4:6], ORDER[6:]]))
    got = [swap(sent[0], "yh")]
    terms = first_terms(after(place, sent[0]), (4, 5, 6, 7))
    down, up, *terms = join(down, up, *terms)
    down, up = add(down, terms[0]), add(up, terms[1])
    down, up = join(down, up)

    here = after(place, down)
    down, up = shift(down, -1), shift(up, 1)
    (kept,) = make(here, 1, (1, Z), [lambda i, s: (s[0], 0)], [ORDER])
    down, up, near, kept, got[0] = join(down, up, near, kept, got[0])
    down = add(down, terms[2])
    down, sent[1], near = join(down, sent[1], near)

    near = near.reshape(2 * Z, -1, near.shape[-1])
    down = shift(down, -1)
    got.append(swap(sent[1], "yh"))
    context = attend(place, queries, doc_ids, near, swap(near, "c"))
    down, context = join(down, context)
    first = add(down, up, terms[3])

    def second_term(order):
        piece = 0 if order < 4 else order // 2 - 1
        return kept[order], got[piece][order if order < 4 else order % 2]

    going = chunk_of(first, 1 - high)
    down, up = add(*second_term(0)), add(*second_term(1))
    down, up, going = join(down, up, going)
    down, up, moved = shift(down, -1), shift(up, 1), swap(going, "yh")
    residual = lax.all_to_all(context, EXP, split_axis=0, concat_axis=1, tiled=True)
    down, up, got[1] = join(down, up, got[1])
    down, up = add(down, *second_term(2)), add(up, *second_term(3))
    down, up, sent[2] = join(down, up, sent[2])
    down, up = shift(down, -1), shift(up, 1)
    got.append(swap(sent[2], "yh"))
    down, up, moved = join(down, up, moved)
    down, up = add(down, *second_term(4)), add(up, *second_term(5))
    down, up = join(down, up)
    down, up = shift(down, -1), shift(up, 1)
    down, up, got[2] = join(down, up, got[2])
    down = add(down, *second_term(6))
    first = add(chunk_of(first, high), after(moved, residual))
    down, residual = join(shift(down, -1), residual)
    second = add(down, up, *second_term(7))

    tokens = routes.shape[0]
    capacity = first.shape[0] // (2 * EXPERTS)
    mix = mixing(routes, route_weights, capacity)
    unit = (jnp.arange(SPLIT)[:, None] == jnp.arange(SPLIT)[None, :]).astype(mix.dtype)
    mix = (mix[None, :, :, None] * unit[:, None, None, :]).reshape(SPLIT * 2 * tokens, -1)
    rows = jnp.concatenate([first, second], axis=1).reshape(2 * EXPERTS, capacity * SPLIT, -1)
    home = lax.all_to_all(rows, ("c",) + EXP, split_axis=0, concat_axis=0, tiled=True)
    home = home.reshape(2, EXPERTS * capacity * SPLIT, -1)
    both = jnp.einsum("tr,crn->ctn", mix, home, preferred_element_type=jnp.float32)
    both = both.reshape(2, SPLIT, 2 * tokens, -1)
    mixed = (both[:, :, :tokens] + both[:, :, tokens:]).transpose(2, 0, 1, 3).reshape(tokens, -1)
    moe_out = residual.astype(jnp.float32) + mixed
    return (context, moe_out.astype(jnp.bfloat16))


def chunk_of(array, at):
    return lax.dynamic_index_in_dim(array, at, 0, keepdims=False)


def mixing(routes, route_weights, capacity):
    flat = routes.reshape(-1)
    pairs = jnp.arange(flat.shape[0])
    same = (flat[:, None] == flat[None, :]) & (pairs[None, :] < pairs[:, None])
    slot = jnp.sum(same.astype(jnp.int32), axis=1).reshape(routes.shape)
    row = routes * capacity + slot
    hit = row[:, :, None] == jnp.arange(EXPERTS * capacity)[None, None, :]
    mix = jnp.sum(jnp.where(hit, route_weights[:, :, None], 0.0), axis=1)
    coarse = mix.astype(jnp.bfloat16)
    fine = (mix - coarse.astype(jnp.float32)).astype(jnp.bfloat16)
    return jnp.concatenate([coarse, fine], axis=0)


def solution(mesh):
    inner = Mesh(mesh.devices.reshape(SHAPE), AXES)
    in_specs = (
        P(CTX, EXP),
        P(CTX, EXP, None),
        P(CTX),
        P(EXP, None, CTX),
        P(EXP, CTX, None),
        P(CTX + EXP, None),
        P(CTX + EXP, None),
    )
    out_specs = (P(CTX, EXP), P(CTX + EXP, None))
    return jax.shard_map(shards, mesh=inner, in_specs=in_specs, out_specs=out_specs, check_vma=False)
```
